32 devices in a mesh: group: 4 (over y, x), tile: 4 (over z), video: 2 (over core).
Axes of the slice: x: 2, y: 2, z: 4, core: 2. Of those that a mesh axis runs over, the one named last changes fastest.
Arguments:
- features: bfloat16 [8, 8, 16, 24, 384], P(('video', 'tile'), 'group'), parts along dimension 0, may hold values from -6 to 6
- group_slot: int32 [4], replicated, may hold values from 0 to 3, each once
- margins: int32 [4, 4], P('tile'), may hold values from 0 to 4, as said below
- norm_gain: float32 [384], replicated, may hold values from 0.1 to 1.9
- kernel: bfloat16 [3, 3, 3, 384, 384], replicated, may hold values from -0.0625 to 0.0625
- conv_bias: float32 [384], replicated, may hold values from -3 to 3
Outputs:
- decoded: bfloat16 [8, 8, 16, 24, 384], P(('video', 'tile'), 'group'), parts along dimension 0
The draws below stay inside these ranges and needn't reach their ends.
There are 2 independent parts, one for each index of `video`. The reference program is written for one: setup_inputs(seed, part) draws one part's arguments, and reference() takes and returns one part's arrays. A program takes and returns all parts, laid end to end along the dimension named above; an argument that names none is the same for every part. Nothing has to cross between parts.
Inputs may be any that keep to these rules, and one draw needn't show every extreme that they name: group_slot is a permutation of 0 to 3. margins[t] is (left, right, up, down) of tile t; a margin is 0 exactly at the image's border and 1 to 4 elsewhere; the margin a tile has toward a neighbour equals the neighbour's margin back; left and right margins depend only on the tile's column, up and down margins are the same for all columns; some margin equals 4.
All inputs are finite; a program needn't handle non-finite values.
Results may differ from the reference program's by a relative error of at most 0.0043.
Values may be sent and summed in bfloat16 or wider, within the bound.
A program may use at most 128 MiB of HBM per device.

```python
import jax
import jax.numpy as jnp
from jax import lax

C = 384
F = 2
CH = 16
CW = 24
M = 4
GRID_R = 2
FRAMES = 8
N_GROUP = 4
N_TILE = 4


def draw_margins(key, part):
    key_cols, key_rows, key_pick = jax.random.split(key, 3)
    boundaries = N_TILE // GRID_R - 1
    widths = jax.random.randint(key_cols, (boundaries,), 1, M + 1).astype(jnp.int32)
    picked = jax.random.randint(key_pick, (), 0, boundaries)
    widths = jnp.where(jnp.arange(boundaries) == picked, jnp.int32(M), widths)
    height = jax.random.randint(key_rows, (), 1, M + 1).astype(jnp.int32)
    nothing = jnp.zeros((1,), jnp.int32)
    left_cols = jnp.concatenate([nothing, widths])
    right_cols = jnp.concatenate([widths, nothing])
    tile_rows = jnp.arange(N_TILE) // (N_TILE // GRID_R)
    tile_cols = jnp.arange(N_TILE) % (N_TILE // GRID_R)
    left_side = left_cols[tile_cols]
    right_side = right_cols[tile_cols]
    upper = jnp.where(tile_rows > 0, height, 0)
    lower = jnp.where(tile_rows < GRID_R - 1, height, 0)
    return jnp.stack([left_side, right_side, upper, lower], axis=1).astype(jnp.int32)


def block_scale(key, extent, pieces, low, largest):
    def one(dim, parts):
        heights = jax.random.uniform(jax.random.fold_in(jax.random.fold_in(key, 6), dim), (parts,), jnp.float32, low / len(pieces), largest / len(pieces))
        return jnp.repeat(jnp.exp(heights), extent[dim] // parts).reshape((-1,) + (1,) * (len(extent) - dim - 1))

    loudness = one(*pieces[0])
    for cut in pieces[1:]:
        loudness = loudness * one(*cut)
    return loudness


def noise(key, dims, spread, most, cuts=(), kind=jnp.bfloat16):
    gain = block_scale(key, dims, cuts, -0.22, 0.18) if cuts else 1.0
    result = jax.random.normal(key, dims, jnp.float32) * spread * gain
    return jnp.minimum(jnp.maximum(result, -most), most).astype(kind)


def setup_inputs(seed: int = 0, part: int = 0) -> dict:
    streams_of = jax.random.split(jax.random.key(seed), 7)
    part_keys = jax.random.split(jax.random.fold_in(streams_of[6], part), 7)
    return {
        "features": noise(part_keys[0], (N_TILE, FRAMES, CH, CW, C), 1.0, 6.0, ((0, 4), (1, 4))),
        "group_slot": jax.random.permutation(streams_of[1], N_GROUP).astype(jnp.int32),
        "margins": draw_margins(jax.random.fold_in(streams_of[6], 71), part),
        "norm_gain": jnp.clip(1.0 + 0.18 * jax.random.normal(streams_of[3], (C,), jnp.float32), 0.1, 1.9),
        "kernel": noise(streams_of[4], (3, 3, 3, C, C), (27 * C) ** -0.5, 0.0625),
        "conv_bias": noise(streams_of[5], (C,), 0.5, 3.0, (), jnp.float32),
    }


def activate(values, norm_gain):
    widened = values.astype(jnp.float32)
    inv_norm = lax.rsqrt(lax.optimization_barrier(jnp.mean(widened * widened, axis=-1, keepdims=True)) + 1e-06)
    return jax.nn.silu(widened * inv_norm * norm_gain).astype(jnp.bfloat16)

def convolve(padded, kernel, conv_bias, row_count, col_count):
    frame_count = padded.shape[0] - 2
    channels = padded.shape[-1]
    summed = jnp.zeros((frame_count * row_count * col_count, kernel.shape[-1]), jnp.float32)
    for tap_time in range(3):
        for tap_row in range(3):
            window = padded[tap_time:tap_time + frame_count, tap_row:tap_row + row_count]
            stacked = jnp.concatenate([window[:, :, tap_col:tap_col + col_count] for tap_col in range(3)], axis=-1)
            flattened = stacked.reshape(frame_count * row_count * col_count, 3 * channels)
            summed = summed + jnp.dot(flattened, kernel[tap_time, tap_row].reshape(3 * channels, -1), preferred_element_type=jnp.float32)
    return summed.reshape(frame_count, row_count, col_count, -1) + conv_bias

def window_band(step, core, near, far):
    position = jnp.arange(core + 2 * M, dtype=jnp.int32)
    if step == 1:
        return position < M + near
    if step == -1:
        return position >= M + core - far
    return (position >= M - near) & (position < M + core + far)

def rim_weight(step, core, near, far):
    position = jnp.arange(core, dtype=jnp.int32)
    if step == 1:
        distance = position + 1
        margin = near
    elif step == -1:
        distance = core - position
        margin = far
    else:
        return jnp.ones((core,), jnp.float32)
    margin_f = margin.astype(jnp.float32)
    return jnp.maximum(margin_f + 1.0 - distance.astype(jnp.float32), 0.0) / (margin_f + 1.0)

def panel_source(step, core):
    if step == 1:
        return (M + core, M, 0)
    if step == -1:
        return (0, M, core - M)
    return (M, core, 0)

def blend_add(weighted, weight_sum, panel, step_r, step_c, row_dest, col_dest, reaches):
    core_h = weighted.shape[1]
    core_w = weighted.shape[2]
    row_len = panel.shape[1]
    col_len = panel.shape[2]
    placed = jnp.pad(panel.astype(jnp.float32), ((0, 0), (row_dest, core_h - row_dest - row_len), (col_dest, core_w - col_dest - col_len), (0, 0)))
    weight = rim_weight(step_r, core_h, reaches[2], reaches[3])[:, None] * rim_weight(step_c, core_w, reaches[0], reaches[1])[None, :]
    return (weighted + placed * weight[None, :, :, None], weight_sum + weight)

def reference(features, group_slot, margins, norm_gain, kernel, conv_bias):
    tile_count, frames_all, core_h, core_w, channels = features.shape
    grid_cols = tile_count // GRID_R
    by_slot = jnp.argsort(group_slot).astype(jnp.int32)
    blocks = features.reshape(tile_count, N_GROUP, F, core_h, core_w, channels)[:, by_slot]
    timeline = blocks.reshape(GRID_R, grid_cols, frames_all, core_h, core_w, channels)
    timeline = timeline.transpose(2, 0, 3, 1, 4, 5).reshape(frames_all, GRID_R * core_h, grid_cols * core_w, channels)
    activated = jnp.pad(activate(timeline, norm_gain), ((0, 0), (M, M), (M, M), (0, 0)))
    buffer_h = core_h + 2 * M
    buffer_w = core_w + 2 * M

    def tile_conv(tile_index):
        tile_row = (tile_index // grid_cols).astype(jnp.int32)
        tile_col = (tile_index % grid_cols).astype(jnp.int32)
        reaches = margins[tile_index]
        region = lax.dynamic_slice(activated, (jnp.int32(0), tile_row * core_h, tile_col * core_w, jnp.int32(0)), (frames_all, buffer_h, buffer_w, channels))
        inside = window_band(0, core_h, reaches[2], reaches[3])[:, None] & window_band(0, core_w, reaches[0], reaches[1])[None, :]
        region = jnp.where(inside[None, :, :, None], region, jnp.zeros_like(region))
        padded = jnp.pad(region, ((2, 0), (1, 1), (1, 1), (0, 0)))
        return convolve(padded, kernel, conv_bias, buffer_h, buffer_w).astype(jnp.bfloat16)
    tile_outputs = lax.map(tile_conv, jnp.arange(tile_count, dtype=jnp.int32))

    def tile_blend(tile_index):
        reaches = margins[tile_index]
        weighted = jnp.zeros((frames_all, core_h, core_w, channels), jnp.float32)
        weight_sum = jnp.zeros((core_h, core_w), jnp.float32)
        for step_r in (1, 0, -1):
            for step_c in (1, 0, -1):
                source = jnp.clip(tile_index - (step_r * grid_cols + step_c), 0, tile_count - 1)
                outputs = tile_outputs[source]
                row_first, row_len, row_dest = panel_source(step_r, core_h)
                col_first, col_len, col_dest = panel_source(step_c, core_w)
                panel = outputs[:, row_first:row_first + row_len, col_first:col_first + col_len]
                weighted, weight_sum = blend_add(weighted, weight_sum, panel, step_r, step_c, row_dest, col_dest, reaches)
        return (weighted / weight_sum[None, :, :, None]).astype(jnp.bfloat16)
    blended = lax.map(tile_blend, jnp.arange(tile_count, dtype=jnp.int32))
    blended = blended.reshape(tile_count, N_GROUP, F, core_h, core_w, channels)[:, group_slot]
    return blended.reshape(tile_count, frames_all, core_h, core_w, channels)
```

```python
import functools
import itertools

import jax
import jax.numpy as jnp
from jax import lax
from jax.experimental import pallas as pl
from jax.experimental.pallas import tpu as pltpu
from jax.sharding import PartitionSpec as P

GRID_R = 2
M = 4
MESH = pl.DeviceIdType.MESH
DIRS = ((-1, 0), (1, 0), (0, -1), (0, 1), (-1, -1), (-1, 1), (1, -1), (1, 1))


def activate(values, gain):
    widened = values.astype(jnp.float32)
    inv_norm = lax.rsqrt(jnp.mean(widened * widened, axis=-1, keepdims=True) + 1e-06)
    half = widened * inv_norm * (0.5 * gain)
    return half + half * jnp.tanh(half)


def table(index, values):
    out = jnp.int32(values[0])
    for k in range(1, len(values)):
        out = jnp.where(index == k, jnp.int32(values[k]), out)
    return out


def body(order, n_tile, slot_ref, margin_ref, x_hbm, gain_ref, bias_ref, w_hbm, out_ref,
         x_ref, prev, rows_in, cols_in, corners_in, cols_out, w, act, z, edge, acc,
         send_small, recv_small, send_big, recv_big, w_sem, x_sem):
    frames, core_h, core_w, channels = x_ref.shape
    n_group = len(order)
    grid_cols = n_tile // GRID_R
    lanes = channels // 128
    pitch = core_w + 16
    cut = core_w - 8
    pieces = ((0, cut), (cut, core_w))
    group = lax.axis_index("group")
    tile = lax.axis_index("tile")
    tile_row = tile // grid_cols
    tile_col = tile % grid_cols
    following = [0] * n_group
    preceding = [0] * n_group
    for k in range(n_group):
        following[order[k]] = order[(k + 1) % n_group]
        preceding[order[(k + 1) % n_group]] = order[k]
    nxt = table(group, following)
    before = table(group, preceding)

    def present(step_r, step_c):
        ok = None
        for at, step, most in ((tile_row, step_r, GRID_R), (tile_col, step_c, grid_cols)):
            if step == 0:
                continue
            here = (at > 0) if step < 0 else (at < most - 1)
            ok = here if ok is None else jnp.logical_and(ok, here)
        return ok

    barrier = pltpu.get_barrier_semaphore()
    greeted = jnp.int32(2)
    for peer in (nxt, before):
        pl.semaphore_signal(barrier, inc=1, device_id={"group": peer}, device_id_type=MESH)
    for step_r, step_c in DIRS:
        ok = present(step_r, step_c)
        greeted = greeted + 3 * ok.astype(jnp.int32)

        @pl.when(ok)
        def _():
            other = tile + step_r * grid_cols + step_c
            for peer in (group, nxt, before):
                pl.semaphore_signal(barrier, inc=1, device_id={"group": peer, "tile": other},
                                    device_id_type=MESH)

    x_copy = pltpu.make_async_copy(x_hbm, x_ref, x_sem)
    x_copy.start()

    def w_copy(a):
        return pltpu.make_async_copy(w_hbm.at[a], w.at[:, pl.ds((2 - a) * channels, channels)], w_sem.at[a])

    for a in (2, 1, 0):
        w_copy(a).start()

    def rim_copy(kind, n):
        step_r, step_c = DIRS[n]
        peer = nxt if kind else group
        other = tile + step_r * grid_cols + step_c
        if step_c == 0:
            src = x_hbm.at[:, 0 if step_r < 0 else core_h - 1]
            dst = rows_in.at[kind, 1 if step_r < 0 else 0]
        elif step_r == 0:
            src = cols_out.at[0 if step_c < 0 else 1]
            dst = cols_in.at[kind, 1 if step_c < 0 else 0]
        else:
            first = 0 if step_c < 0 else core_w - 8
            src = x_hbm.at[:, 0 if step_r < 0 else core_h - 1, pl.ds(first, 8)]
            dst = corners_in.at[kind, 1 if step_r < 0 else 0, 1 if step_c < 0 else 0]
        return pltpu.make_async_remote_copy(
            src_ref=src, dst_ref=dst, send_sem=send_small.at[kind, n], recv_sem=recv_small.at[kind, n],
            device_id={"group": peer, "tile": other}, device_id_type=MESH)

    def block_copy(f, k):
        cols = pl.ds(pieces[k][0], pieces[k][1] - pieces[k][0])
        return pltpu.make_async_remote_copy(
            src_ref=x_hbm.at[f, :, cols], dst_ref=prev.at[f, :, cols],
            send_sem=send_big.at[f, k], recv_sem=recv_big.at[f, k],
            device_id={"group": nxt}, device_id_type=MESH)

    def send_rims(kind, side):
        for n, (step_r, step_c) in enumerate(DIRS):
            if (step_r == 0) == side:
                @pl.when(present(step_r, step_c))
                def _():
                    rim_copy(kind, n).start()

    def wait_rims(kind):
        for n, (step_r, step_c) in enumerate(DIRS):
            m = DIRS.index((-step_r, -step_c))

            @pl.when(present(step_r, step_c))
            def _():
                rim_copy(kind, m).wait_recv()

    pl.semaphore_wait(barrier, greeted)
    for k in (0, 1):
        block_copy(1, k).start()
    send_rims(0, False)

    zero_rim = jnp.zeros((pitch, 128), jnp.float32)
    for slot in range(2):
        for c in range(lanes):
            act[slot, c, pl.ds(0, pitch)] = zero_rim
            act[slot, c, pl.ds((core_h + 1) * pitch, pitch)] = zero_rim
            act[slot, c, pl.ds(pitch + 7, core_h, stride=pitch)] = zero_rim[:core_h]
            act[slot, c, pl.ds(pitch + 8 + core_w, core_h, stride=pitch)] = zero_rim[:core_h]

    x_copy.wait()
    for f in range(frames):
        side = x_ref[f].astype(jnp.float32)
        cols_out[0, f] = side[:, 0, :].astype(jnp.bfloat16)
        cols_out[1, f] = side[:, core_w - 1, :].astype(jnp.bfloat16)
    send_rims(0, True)
    send_rims(1, False)
    send_rims(1, True)
    for k in (0, 1):
        block_copy(0, k).start()

    gain = gain_ref[...].reshape(1, channels)
    left, right, up, down = [margin_ref[0, k] for k in range(4)]
    not_first = jnp.where(jnp.full((core_h, channels), slot_ref[group] > 0), 1.0, 0.0)

    def kept(m):
        m_f = jnp.full((core_h, channels), m, jnp.int32).astype(jnp.float32)
        return (m_f + 1.0) / (m_f + 2.0)

    row_at = lax.broadcasted_iota(jnp.int32, (core_h, channels), 0)
    alpha = [jnp.where(row_at == core_h - down, kept(down), 1.0), None,
             jnp.where(row_at == up - 1, kept(up), 1.0)]
    beta_left = kept(left)
    beta_right = kept(right)

    def put_act(slot, at, v):
        for c in range(lanes):
            act[slot, c, at] = v[:, c * 128:(c + 1) * 128]

    def interior(f, source, slot, first, last):
        def some_rows(i, carry):
            for k in range(4):
                at = pl.multiple_of((4 * i + k + 1) * pitch + 8 + first, 8)
                put_act(slot, pl.ds(at, last - first), activate(source[f, 4 * i + k, first:last], gain))
            return carry
        lax.fori_loop(0, core_h // 4, some_rows, 0)

    def rims(kind, f, slot):
        store = functools.partial(put_act, slot)
        for n, (step_r, step_c) in enumerate(DIRS):
            @pl.when(present(step_r, step_c))
            def _():
                vertical = (core_h + 1) * pitch if step_r > 0 else 0
                if step_c == 0:
                    store(pl.ds(vertical + 8, core_w), activate(rows_in[kind, 1 if step_r > 0 else 0, f], gain))
                elif step_r == 0:
                    start = pitch + (8 + core_w if step_c > 0 else 7)
                    store(pl.ds(start, core_h, stride=pitch),
                          activate(cols_in[kind, 1 if step_c > 0 else 0, f], gain))
                else:
                    v = activate(corners_in[kind, 1 if step_r > 0 else 0, 1 if step_c > 0 else 0, f], gain)
                    at = vertical + (8 + core_w if step_c > 0 else 7)
                    store(pl.ds(at, 1), v[0:1] if step_c > 0 else v[7:8])

    def column(kind, slot, b, p):
        at = pl.ds(b * pitch + 7 + p, core_h, stride=pitch)
        v = jnp.concatenate([act[slot, c, at] for c in range(lanes)], axis=-1)
        if alpha[b] is not None:
            v = v * alpha[b]
        return v * not_first if kind else v

    def spread(kind, slot, first, last):
        def one_col(p, carry):
            for b in range(3):
                z[slot, b, pl.ds(pl.multiple_of(p * core_h, core_h), core_h)] = column(kind, slot, b, p).astype(jnp.bfloat16)
            return carry
        lax.fori_loop(first, last, one_col, 0, unroll=2)

    def spread_left(kind, slot):
        for j in range(M):
            for b in range(3):
                v = column(kind, slot, b, j + 2)
                edge[slot, b, 1, j * core_h:(j + 1) * core_h] = jnp.where(j == left - 1, v * beta_left, v).astype(jnp.bfloat16)

    def spread_right(kind, slot):
        for j in range(M):
            for b in range(3):
                v = column(kind, slot, b, core_w - M + j)
                edge[slot, b, 0, j * core_h:(j + 1) * core_h] = jnp.where(M - j == right, v * beta_right, v).astype(jnp.bfloat16)

    def spread_all(kind, slot):
        spread(kind, slot, 0, core_w + 2)
        spread_left(kind, slot)
        spread_right(kind, slot)

    def windows(slot, j0, j1):
        def rows(ref, first, last):
            return ref[first * core_h:last * core_h]
        out = []
        for b in range(3):
            plain = z.at[slot, b]
            inner = min(j1, core_w - M)
            near = [rows(plain, j0, inner)]
            if j1 > inner:
                near.append(rows(edge.at[slot, b, 0], 0, j1 - inner))
            outer = max(j0, M)
            far = [rows(edge.at[slot, b, 1], j0, M)] if j0 < M else []
            far.append(rows(plain, outer + 2, j1 + 2))
            out += [jnp.concatenate(near, axis=0), rows(plain, j0 + 1, j1 + 1), jnp.concatenate(far, axis=0)]
        return jnp.concatenate(out, axis=-1)

    def multiply(slot, tap, target, many, j0, j1, add):
        r = jnp.dot(windows(slot, j0, j1), w[:, tap * channels:(tap + many) * channels],
                    preferred_element_type=jnp.float32)
        at = slice(j0 * core_h, j1 * core_h)
        for c in range(many * lanes):
            v = r[:, c * 128:(c + 1) * 128]
            acc[target * lanes + c, at] = acc[target * lanes + c, at] + v if add else v

    bias = bias_ref[...].reshape(1, channels)

    def give(s, first, last):
        def put(i, carry):
            v = jnp.concatenate([acc[s * lanes + c, pl.ds(i + first * core_h, last - first, stride=core_h)]
                                 for c in range(lanes)], axis=-1)
            out_ref[s, i, first:last] = (v + bias).astype(out_ref.dtype)
            return carry
        lax.fori_loop(0, core_h, put, 0, unroll=4)

    interior(0, x_ref, 0, 0, core_w)
    interior(1, x_ref, 1, 0, core_w)
    wait_rims(0)
    for f in (0, 1):
        rims(0, f, f)
        spread_all(0, f)
    w_copy(2).wait()
    w_copy(1).wait()
    multiply(0, 0, 0, 2, 0, core_w, False)
    multiply(1, 0, 1, 1, 0, core_w, True)

    for k, (first, last) in enumerate(pieces):
        block_copy(1, k).wait_recv()
        interior(1, prev, 1, first, last)
    wait_rims(1)
    rims(1, 1, 1)
    spread_all(1, 1)
    w_copy(0).wait()
    multiply(1, 1, 0, 2, 0, core_w, True)
    give(1, 0, core_w)

    block_copy(0, 0).wait_recv()
    interior(0, prev, 0, 0, cut)
    rims(1, 0, 0)
    spread(1, 0, 0, cut + 1)
    spread_left(1, 0)
    multiply(0, 2, 0, 1, 0, cut - 1, True)
    give(0, 0, cut - 8)
    block_copy(0, 1).wait_recv()
    interior(0, prev, 0, cut, core_w)
    spread(1, 0, cut + 1, core_w + 2)
    spread_right(1, 0)
    multiply(0, 2, 0, 1, cut - 1, core_w, True)
    give(0, cut - 8, core_w)

    for kind in (0, 1):
        for n, (step_r, step_c) in enumerate(DIRS):
            @pl.when(present(step_r, step_c))
            def _():
                rim_copy(kind, n).wait_send()
    for f in (1, 0):
        for k in (0, 1):
            block_copy(f, k).wait_send()


def pick(orders, slot_ref, branch_ref):
    n_group = len(orders[0])
    rel = [lax.rem(slot_ref[d] - slot_ref[0] + n_group, n_group) for d in range(n_group)]
    branch = jnp.int32(0)
    for k, order in enumerate(orders):
        hit = jnp.bool_(True)
        for position, device in enumerate(order):
            hit = jnp.logical_and(hit, rel[device] == position)
        branch = jnp.where(hit, jnp.int32(k), branch)
    branch_ref[0] = branch


def local(orders, n_tile, features, group_slot, margins, norm_gain, kernel, conv_bias):
    x = features[0]
    frames, core_h, core_w, channels = x.shape
    weights = kernel.reshape(3, 9 * channels, channels)
    branch = pl.pallas_call(
        functools.partial(pick, orders),
        out_shape=jax.ShapeDtypeStruct((1,), jnp.int32),
        in_specs=[pl.BlockSpec(memory_space=pltpu.SMEM)],
        out_specs=pl.BlockSpec(memory_space=pltpu.SMEM),
        name="pick",
    )(group_slot)[0]

    pitch = core_w + 16
    vmem = pl.BlockSpec(memory_space=pltpu.VMEM)
    smem = pl.BlockSpec(memory_space=pltpu.SMEM)

    def call(k):
        def run(slot, margin, xx, gain, bias, w):
            return pl.pallas_call(
                functools.partial(body, orders[k], n_tile),
                out_shape=jax.ShapeDtypeStruct(x.shape, jnp.bfloat16),
                in_specs=[smem, smem, pl.BlockSpec(memory_space=pl.ANY), vmem, vmem, pl.BlockSpec(memory_space=pl.ANY)],
                out_specs=vmem,
                scratch_shapes=[
                    pltpu.VMEM((frames, core_h, core_w, channels), jnp.bfloat16),
                    pltpu.VMEM((frames, core_h, core_w, channels), jnp.bfloat16),
                    pltpu.VMEM((2, 2, frames, core_w, channels), jnp.bfloat16),
                    pltpu.VMEM((2, 2, frames, core_h, channels), jnp.bfloat16),
                    pltpu.VMEM((2, 2, 2, frames, 8, channels), jnp.bfloat16),
                    pltpu.VMEM((2, frames, core_h, channels), jnp.bfloat16),
                    pltpu.VMEM((9 * channels, 3 * channels), jnp.bfloat16),
                    pltpu.VMEM((2, channels // 128, (core_h + 2) * pitch, 128), jnp.float32),
                    pltpu.VMEM((2, 3, (core_w + 2) * core_h, channels), jnp.bfloat16),
                    pltpu.VMEM((2, 3, 2, M * core_h, channels), jnp.bfloat16),
                    pltpu.VMEM((2 * channels // 128, core_h * core_w, 128), jnp.float32),
                    pltpu.SemaphoreType.DMA((2, 8)),
                    pltpu.SemaphoreType.DMA((2, 8)),
                    pltpu.SemaphoreType.DMA((2, 2)),
                    pltpu.SemaphoreType.DMA((2, 2)),
                    pltpu.SemaphoreType.DMA((3,)),
                    pltpu.SemaphoreType.DMA,
                ],
                compiler_params=pltpu.CompilerParams(collective_id=k, has_side_effects=True,
                                                     vmem_limit_bytes=40 << 20),
                name="conv_order_%d" % k,
            )(slot, margin, xx, gain, bias, w)
        return run

    out = lax.switch(branch, [call(k) for k in range(len(orders))], group_slot, margins, x,
                     norm_gain, conv_bias, weights)
    return out[None]


def solution(mesh):
    n_group = mesh.shape["group"]
    n_tile = mesh.shape["tile"]
    orders = [(0,) + rest for rest in itertools.permutations(range(1, n_group))]
    return jax.shard_map(
        functools.partial(local, orders, n_tile),
        mesh=mesh,
        in_specs=(
            P(("video", "tile"), "group", None, None, None),
            P(),
            P("tile", None),
            P(),
            P(),
            P(),
        ),
        out_specs=P(("video", "tile"), "group", None, None, None),
        check_vma=False,
    )
```

```python
import functools

import jax
import jax.numpy as jnp
from jax import lax
from jax.experimental import pallas as pl
from jax.experimental.pallas import tpu as pltpu
from jax.sharding import PartitionSpec as P

GRID_R = 2
M = 4
MESH = pl.DeviceIdType.MESH
DIRS = ((-1, 0), (1, 0), (0, -1), (0, 1), (-1, -1), (-1, 1), (1, -1), (1, 1))


def activate(values, gain):
    widened = values.astype(jnp.float32)
    inv_norm = lax.rsqrt(jnp.mean(widened * widened, axis=-1, keepdims=True) + 1e-06)
    half = widened * inv_norm * (0.5 * gain)
    return half + half * jnp.tanh(half)


def body(n_group, n_tile, slot_ref, margin_ref, x_hbm, gain_ref, bias_ref, w_hbm, out_ref,
         x_ref, first_in, second_in, relay, rows_in, cols_in, corners_in, cols_out, w, act, z, edge, acc,
         send_small, recv_small, send_big, recv_big, w_sem, x_sem):
    frames, core_h, core_w, channels = x_ref.shape
    grid_cols = n_tile // GRID_R
    lanes = channels // 128
    pitch = core_w + 16
    half = core_h // 2
    cut = core_w - 8
    pieces = ((0, cut), (cut, core_w))
    group = lax.axis_index("group")
    tile = lax.axis_index("tile")
    tile_row = tile // grid_cols
    tile_col = tile % grid_cols
    partners = (group + 1 - 2 * (group % 2), (group + n_group // 2) % n_group)

    def present(step_r, step_c):
        ok = None
        for at, step, most in ((tile_row, step_r, GRID_R), (tile_col, step_c, grid_cols)):
            if step == 0:
                continue
            here = (at > 0) if step < 0 else (at < most - 1)
            ok = here if ok is None else jnp.logical_and(ok, here)
        return ok

    barrier = pltpu.get_barrier_semaphore()
    greeted = jnp.int32(2)
    for peer in partners:
        pl.semaphore_signal(barrier, inc=1, device_id={"group": peer}, device_id_type=MESH)
    for step_r, step_c in DIRS:
        ok = present(step_r, step_c)
        greeted = greeted + ok.astype(jnp.int32)

        @pl.when(ok)
        def _():
            pl.semaphore_signal(barrier, inc=1, device_id={"tile": tile + step_r * grid_cols + step_c},
                                device_id_type=MESH)

    x_copy = pltpu.make_async_copy(x_hbm, x_ref, x_sem)
    x_copy.start()

    def w_copy(a):
        return pltpu.make_async_copy(w_hbm.at[a], w.at[:, pl.ds((2 - a) * channels, channels)], w_sem.at[a])

    for a in (2, 1, 0):
        w_copy(a).start()

    def rim_at(stage, n):
        step_r, step_c = DIRS[n]
        if step_c == 0:
            return rows_in.at[stage, 1 if step_r > 0 else 0]
        if step_r == 0:
            return cols_in.at[stage, 1 if step_c > 0 else 0]
        return corners_in.at[stage, 1 if step_r > 0 else 0, 1 if step_c > 0 else 0]

    def rim_copy(n):
        step_r, step_c = DIRS[n]
        row = 0 if step_r < 0 else core_h - 1
        if step_c == 0:
            src = x_hbm.at[:, row]
        elif step_r == 0:
            src = cols_out.at[0 if step_c < 0 else 1]
        else:
            src = x_hbm.at[:, row, pl.ds(0 if step_c < 0 else core_w - 8, 8)]
        return pltpu.make_async_remote_copy(
            src_ref=src, dst_ref=rim_at(0, DIRS.index((-step_r, -step_c))),
            send_sem=send_small.at[0, n], recv_sem=recv_small.at[0, n],
            device_id={"tile": tile + step_r * grid_cols + step_c}, device_id_type=MESH)

    def way(n):
        return 0 if DIRS[n][1] == 0 else 1

    def rim_pass(phase, n):
        return pltpu.make_async_remote_copy(
            src_ref=rim_at(0 if phase == 1 else 3, n), dst_ref=rim_at(phase, n),
            send_sem=send_small.at[phase, n], recv_sem=recv_small.at[phase, n],
            device_id={"group": partners[way(n) if phase == 1 else 1 - way(n)]}, device_id_type=MESH)

    def block_pass(phase, f, k, h):
        cols = pl.ds(pieces[k][0], pieces[k][1] - pieces[k][0])
        rows = pl.ds(h * half, half)
        return pltpu.make_async_remote_copy(
            src_ref=(x_hbm if phase == 1 else relay).at[f, rows, cols],
            dst_ref=(first_in if phase == 1 else second_in).at[f, rows, cols],
            send_sem=send_big.at[phase - 1, f, 2 * k + h], recv_sem=recv_big.at[phase - 1, f, 2 * k + h],
            device_id={"group": partners[h if phase == 1 else 1 - h]}, device_id_type=MESH)

    def for_dirs(act_on, side=None):
        for n, (step_r, step_c) in enumerate(DIRS):
            if side is None or (step_r == 0) == side:
                pl.when(present(step_r, step_c))(functools.partial(act_on, n))

    def opposite(n):
        return DIRS.index((-DIRS[n][0], -DIRS[n][1]))

    pl.semaphore_wait(barrier, greeted)
    for_dirs(lambda n: rim_copy(n).start(), False)
    for k in (0, 1):
        for h in (0, 1):
            block_pass(1, 1, k, h).start()

    zero_rim = jnp.zeros((pitch, 128), jnp.float32)
    for slot in range(2):
        for c in range(lanes):
            act[slot, c, pl.ds(0, pitch)] = zero_rim
            act[slot, c, pl.ds((core_h + 1) * pitch, pitch)] = zero_rim
            act[slot, c, pl.ds(pitch + 7, core_h, stride=pitch)] = zero_rim[:core_h]
            act[slot, c, pl.ds(pitch + 8 + core_w, core_h, stride=pitch)] = zero_rim[:core_h]

    x_copy.wait()
    for f in range(frames):
        side = x_ref[f].astype(jnp.float32)
        cols_out[0, f] = side[:, 0, :].astype(jnp.bfloat16)
        cols_out[1, f] = side[:, core_w - 1, :].astype(jnp.bfloat16)
    for_dirs(lambda n: rim_copy(n).start(), True)

    gain = gain_ref[...].reshape(1, channels)
    left, right, up, down = [margin_ref[0, k] for k in range(4)]
    place = slot_ref[group]
    places = [slot_ref[p] for p in partners]
    mine = [jnp.full((1, channels), places[h] == place - 1) for h in (0, 1)]
    theirs = [jnp.full((1, channels), places[h] == places[1 - h] - 1) for h in (0, 1)]

    def choose(hit, a, b):
        return jnp.where(hit, a.astype(jnp.float32), b.astype(jnp.float32))

    not_first = jnp.where(jnp.full((core_h, channels), place > 0), 1.0, 0.0)

    def kept(m):
        m_f = jnp.full((core_h, channels), m, jnp.int32).astype(jnp.float32)
        return (m_f + 1.0) / (m_f + 2.0)

    row_at = lax.broadcasted_iota(jnp.int32, (core_h, channels), 0)
    alpha = [jnp.where(row_at == core_h - down, kept(down), 1.0), None,
             jnp.where(row_at == up - 1, kept(up), 1.0)]
    beta_left = kept(left)
    beta_right = kept(right)

    def put_act(slot, at, v):
        for c in range(lanes):
            act[slot, c, at] = v[:, c * 128:(c + 1) * 128]

    def interior(kind, f, slot, first, last):
        def some_rows(i, carry):
            for h in (0, 1):
                for k in range(2):
                    row = h * half + 2 * i + k
                    if kind:
                        v = choose(mine[h], first_in[f, row, first:last], second_in[f, row, first:last])
                    else:
                        v = x_ref[f, row, first:last]
                    at = pl.multiple_of((row + 1) * pitch + 8 + first, 8)
                    put_act(slot, pl.ds(at, last - first), activate(v, gain))
            return carry
        lax.fori_loop(0, half // 2, some_rows, 0)

    def forward(f, k):
        first, last = pieces[k]
        for h in (0, 1):
            block_pass(1, f, k, h).wait_recv()

        def some_rows(i, carry):
            for h in (0, 1):
                row = h * half + i
                relay[f, row, first:last] = choose(theirs[h], first_in[f, row, first:last],
                                                   x_ref[f, row, first:last]).astype(jnp.bfloat16)
            return carry
        lax.fori_loop(0, half, some_rows, 0, unroll=2)
        for h in (0, 1):
            block_pass(2, f, k, h).start()

    def forward_rim(n):
        rim_pass(1, n).wait_recv()
        hit = theirs[way(n)]
        for f in range(frames):
            rim_at(3, n)[f] = choose(hit, rim_at(1, n)[f], rim_at(0, n)[f]).astype(jnp.bfloat16)
        rim_pass(2, n).start()

    def rims(kind, f, slot):
        store = functools.partial(put_act, slot)

        def one(n):
            step_r, step_c = DIRS[n]
            if kind:
                v = choose(mine[way(n)], rim_at(1, n)[f], rim_at(2, n)[f])
            else:
                v = rim_at(0, n)[f]
            v = activate(v, gain)
            vertical = (core_h + 1) * pitch if step_r > 0 else 0
            if step_c == 0:
                store(pl.ds(vertical + 8, core_w), v)
            elif step_r == 0:
                store(pl.ds(pitch + (8 + core_w if step_c > 0 else 7), core_h, stride=pitch), v)
            else:
                store(pl.ds(vertical + (8 + core_w if step_c > 0 else 7), 1), v[0:1] if step_c > 0 else v[7:8])
        for_dirs(one)

    def column(kind, slot, b, p):
        at = pl.ds(b * pitch + 7 + p, core_h, stride=pitch)
        v = jnp.concatenate([act[slot, c, at] for c in range(lanes)], axis=-1)
        if alpha[b] is not None:
            v = v * alpha[b]
        return v * not_first if kind else v

    def spread(kind, slot, first, last):
        def one_col(p, carry):
            for b in range(3):
                z[slot, b, pl.ds(pl.multiple_of(p * core_h, core_h), core_h)] = column(kind, slot, b, p).astype(jnp.bfloat16)
            return carry
        lax.fori_loop(first, last, one_col, 0, unroll=2)

    def spread_left(kind, slot):
        for j in range(M):
            for b in range(3):
                v = column(kind, slot, b, j + 2)
                edge[slot, b, 1, j * core_h:(j + 1) * core_h] = jnp.where(j == left - 1, v * beta_left, v).astype(jnp.bfloat16)

    def spread_right(kind, slot):
        for j in range(M):
            for b in range(3):
                v = column(kind, slot, b, core_w - M + j)
                edge[slot, b, 0, j * core_h:(j + 1) * core_h] = jnp.where(M - j == right, v * beta_right, v).astype(jnp.bfloat16)

    def spread_all(kind, slot):
        spread(kind, slot, 0, core_w + 2)
        spread_left(kind, slot)
        spread_right(kind, slot)

    def windows(slot, j0, j1):
        def rows(ref, first, last):
            return ref[first * core_h:last * core_h]
        out = []
        for b in range(3):
            plain = z.at[slot, b]
            inner = min(j1, core_w - M)
            near = [rows(plain, j0, inner)]
            if j1 > inner:
                near.append(rows(edge.at[slot, b, 0], 0, j1 - inner))
            outer = max(j0, M)
            far = [rows(edge.at[slot, b, 1], j0, M)] if j0 < M else []
            far.append(rows(plain, outer + 2, j1 + 2))
            out += [jnp.concatenate(near, axis=0), rows(plain, j0 + 1, j1 + 1), jnp.concatenate(far, axis=0)]
        return jnp.concatenate(out, axis=-1)

    def multiply(slot, tap, target, many, j0, j1, between=None):
        at = slice(j0 * core_h, j1 * core_h)
        steps = many * lanes // 2 if many > 1 else lanes - 1
        stride = 2 if many > 1 else 1

        def step(n, carry):
            first = pl.multiple_of((tap * lanes + stride * n) * 128, 128)
            r = jnp.dot(windows(slot, j0, j1), w[:, pl.ds(first, 256)], preferred_element_type=jnp.float32)
            c = target * lanes + stride * n
            if many > 1:
                acc[c, at] += r[:, :128]
            else:
                @pl.when(n == 0)
                def _():
                    acc[c, at] += r[:, :128]
            acc[c + 1, at] += r[:, 128:]
            if between is not None:
                pl.when(n == 0)(between)
            return carry
        lax.fori_loop(0, steps, step, 0)

    bias = bias_ref[...].reshape(1, channels)

    def give(s, first, last):
        def put(i, carry):
            v = jnp.concatenate([acc[s * lanes + c, pl.ds(i + first * core_h, last - first, stride=core_h)]
                                 for c in range(lanes)], axis=-1)
            out_ref[s, i, first:last] = (v + bias).astype(out_ref.dtype)
            return carry
        lax.fori_loop(0, core_h, put, 0, unroll=4)

    def clear(i, carry):
        acc[i] = jnp.zeros(acc.shape[1:], jnp.float32)
        return carry
    lax.fori_loop(0, 2 * lanes, clear, 0)

    interior(0, 0, 0, 0, core_w)
    interior(0, 1, 1, 0, core_w)
    for_dirs(lambda n: rim_copy(opposite(n)).wait_recv())
    for_dirs(lambda n: rim_pass(1, n).start())
    for f in (0, 1):
        rims(0, f, f)
        spread_all(0, f)
        forward(1, f)
    for_dirs(forward_rim)
    for k in (0, 1):
        for h in (0, 1):
            block_pass(1, 0, k, h).start()
    w_copy(2).wait()
    w_copy(1).wait()
    multiply(0, 0, 0, 2, 0, core_w)
    multiply(1, 0, 1, 1, 0, core_w)

    for k in (0, 1):
        for h in (0, 1):
            block_pass(2, 1, k, h).wait_recv()
    interior(1, 1, 1, 0, core_w)
    for_dirs(lambda n: rim_pass(2, n).wait_recv())
    rims(1, 1, 1)
    spread_all(1, 1)
    forward(0, 0)
    w_copy(0).wait()
    multiply(1, 1, 0, 2, 0, core_w, functools.partial(forward, 0, 1))
    give(1, 0, core_w)

    for h in (0, 1):
        block_pass(2, 0, 0, h).wait_recv()
    interior(1, 0, 0, 0, cut)
    rims(1, 0, 0)
    spread(1, 0, 0, cut + 1)
    spread_left(1, 0)
    multiply(0, 2, 0, 1, 0, cut - 1)
    give(0, 0, cut - 8)
    for h in (0, 1):
        block_pass(2, 0, 1, h).wait_recv()
    interior(1, 0, 0, cut, core_w)
    spread(1, 0, cut + 1, core_w + 2)
    spread_right(1, 0)
    multiply(0, 2, 0, 1, cut - 1, core_w)
    give(0, cut - 8, core_w)

    def sent(n):
        rim_copy(n).wait_send()
        for phase in (1, 2):
            rim_pass(phase, n).wait_send()
    for_dirs(sent)
    for phase in (1, 2):
        for f in (1, 0):
            for k in (0, 1):
                for h in (0, 1):
                    block_pass(phase, f, k, h).wait_send()


def local(n_group, n_tile, features, group_slot, margins, norm_gain, kernel, conv_bias):
    x = features[0]
    frames, core_h, core_w, channels = x.shape
    weights = kernel.reshape(3, 9 * channels, channels)
    pitch = core_w + 16
    block = pltpu.VMEM((frames, core_h, core_w, channels), jnp.bfloat16)
    vmem = pl.BlockSpec(memory_space=pltpu.VMEM)
    smem = pl.BlockSpec(memory_space=pltpu.SMEM)
    anywhere = pl.BlockSpec(memory_space=pl.ANY)
    out = pl.pallas_call(
        functools.partial(body, n_group, n_tile),
        out_shape=jax.ShapeDtypeStruct(x.shape, jnp.bfloat16),
        in_specs=[smem, smem, anywhere, vmem, vmem, anywhere],
        out_specs=vmem,
        scratch_shapes=[
            block, block, block, block,
            pltpu.VMEM((4, 2, frames, core_w, channels), jnp.bfloat16),
            pltpu.VMEM((4, 2, frames, core_h, channels), jnp.bfloat16),
            pltpu.VMEM((4, 2, 2, frames, 8, channels), jnp.bfloat16),
            pltpu.VMEM((2, frames, core_h, channels), jnp.bfloat16),
            pltpu.VMEM((9 * channels, 3 * channels), jnp.bfloat16),
            pltpu.VMEM((2, channels // 128, (core_h + 2) * pitch, 128), jnp.float32),
            pltpu.VMEM((2, 3, (core_w + 2) * core_h, channels), jnp.bfloat16),
            pltpu.VMEM((2, 3, 2, M * core_h, channels), jnp.bfloat16),
            pltpu.VMEM((2 * channels // 128, core_h * core_w, 128), jnp.float32),
            pltpu.SemaphoreType.DMA((3, 8)),
            pltpu.SemaphoreType.DMA((3, 8)),
            pltpu.SemaphoreType.DMA((2, 2, 4)),
            pltpu.SemaphoreType.DMA((2, 2, 4)),
            pltpu.SemaphoreType.DMA((3,)),
            pltpu.SemaphoreType.DMA,
        ],
        compiler_params=pltpu.CompilerParams(collective_id=0, has_side_effects=True, vmem_limit_bytes=40 << 20),
        name="conv",
    )(group_slot, margins, x, norm_gain, conv_bias, weights)
    return out[None]


def solution(mesh):
    n_group = mesh.shape["group"]
    n_tile = mesh.shape["tile"]
    if n_group != 4:
        raise ValueError("group size")
    return jax.shard_map(
        functools.partial(local, n_group, n_tile),
        mesh=mesh,
        in_specs=(
            P(("video", "tile"), "group", None, None, None),
            P(),
            P("tile", None),
            P(),
            P(),
            P(),
        ),
        out_specs=P(("video", "tile"), "group", None, None, None),
        check_vma=False,
    )
```

```python
import functools

import jax
import jax.numpy as jnp
from jax import lax
from jax.experimental import pallas as pl
from jax.experimental.pallas import tpu as pltpu
from jax.sharding import PartitionSpec as P

GRID_R = 2
M = 4
MESH = pl.DeviceIdType.MESH
DIRS = ((-1, 0), (1, 0), (0, -1), (0, 1), (-1, -1), (-1, 1), (1, -1), (1, 1))


def activate(values, gain):
    widened = values.astype(jnp.float32)
    inv_norm = lax.rsqrt(jnp.mean(widened * widened, axis=-1, keepdims=True) + 1e-06)
    half = widened * inv_norm * (0.5 * gain)
    return half + half * jnp.tanh(half)


def body(n_group, n_tile, slot_ref, margin_ref, x_hbm, gain_ref, bias_ref, w_hbm, out_ref,
         x_ref, first_in, second_in, relay, rows_in, cols_in, corners_in, cols_out, w, act, z, edge, acc,
         send_small, recv_small, send_big, recv_big, w_sem, x_sem):
    frames, core_h, core_w, channels = x_ref.shape
    grid_cols = n_tile // GRID_R
    lanes = channels // 128
    pitch = core_w + 16
    half = core_h // 2
    cut = core_w - 8
    pieces = ((0, cut), (cut, core_w))
    group = lax.axis_index("group")
    tile = lax.axis_index("tile")
    tile_row = tile // grid_cols
    tile_col = tile % grid_cols
    partners = (group + 1 - 2 * (group % 2), (group + n_group // 2) % n_group)

    def present(step_r, step_c):
        ok = None
        for at, step, most in ((tile_row, step_r, GRID_R), (tile_col, step_c, grid_cols)):
            if step == 0:
                continue
            here = (at > 0) if step < 0 else (at < most - 1)
            ok = here if ok is None else jnp.logical_and(ok, here)
        return ok

    barrier = pltpu.get_barrier_semaphore()
    greeted = jnp.int32(2)
    for peer in partners:
        pl.semaphore_signal(barrier, inc=1, device_id={"group": peer}, device_id_type=MESH)
    for step_r, step_c in DIRS:
        ok = present(step_r, step_c)
        greeted = greeted + ok.astype(jnp.int32)

        @pl.when(ok)
        def _():
            pl.semaphore_signal(barrier, inc=1, device_id={"tile": tile + step_r * grid_cols + step_c},
                                device_id_type=MESH)

    x_copy = pltpu.make_async_copy(x_hbm, x_ref, x_sem)
    x_copy.start()

    def w_copy(a):
        return pltpu.make_async_copy(w_hbm.at[a], w.at[:, pl.ds((2 - a) * channels, channels)], w_sem.at[a])

    for a in (2, 1, 0):
        w_copy(a).start()

    def rim_at(stage, n):
        step_r, step_c = DIRS[n]
        if step_c == 0:
            return rows_in.at[stage, 1 if step_r > 0 else 0]
        if step_r == 0:
            return cols_in.at[stage, 1 if step_c > 0 else 0]
        return corners_in.at[stage, 1 if step_r > 0 else 0, 1 if step_c > 0 else 0]

    def rim_copy(n):
        step_r, step_c = DIRS[n]
        row = 0 if step_r < 0 else core_h - 1
        if step_c == 0:
            src = x_hbm.at[:, row]
        elif step_r == 0:
            src = cols_out.at[0 if step_c < 0 else 1]
        else:
            src = x_hbm.at[:, row, pl.ds(0 if step_c < 0 else core_w - 8, 8)]
        return pltpu.make_async_remote_copy(
            src_ref=src, dst_ref=rim_at(0, DIRS.index((-step_r, -step_c))),
            send_sem=send_small.at[0, n], recv_sem=recv_small.at[0, n],
            device_id={"tile": tile + step_r * grid_cols + step_c}, device_id_type=MESH)

    def way(n):
        return 0 if DIRS[n][1] == 0 else 1

    def rim_pass(phase, n):
        return pltpu.make_async_remote_copy(
            src_ref=rim_at(0 if phase == 1 else 3, n), dst_ref=rim_at(phase, n),
            send_sem=send_small.at[phase, n], recv_sem=recv_small.at[phase, n],
            device_id={"group": partners[way(n) if phase == 1 else 1 - way(n)]}, device_id_type=MESH)

    def block_pass(phase, f, k, h):
        cols = pl.ds(pieces[k][0], pieces[k][1] - pieces[k][0])
        rows = pl.ds(h * half, half)
        return pltpu.make_async_remote_copy(
            src_ref=(x_hbm if phase == 1 else relay).at[f, rows, cols],
            dst_ref=(first_in if phase == 1 else second_in).at[f, rows, cols],
            send_sem=send_big.at[phase - 1, f, 2 * k + h], recv_sem=recv_big.at[phase - 1, f, 2 * k + h],
            device_id={"group": partners[h if phase == 1 else 1 - h]}, device_id_type=MESH)

    def for_dirs(act_on, side=None):
        for n, (step_r, step_c) in enumerate(DIRS):
            if side is None or (step_r == 0) == side:
                pl.when(present(step_r, step_c))(functools.partial(act_on, n))

    def opposite(n):
        return DIRS.index((-DIRS[n][0], -DIRS[n][1]))

    pl.semaphore_wait(barrier, greeted)
    for_dirs(lambda n: rim_copy(n).start(), False)
    for k in (0, 1):
        for h in (0, 1):
            block_pass(1, 1, k, h).start()
    for h in (0, 1):
        block_pass(1, 0, 0, h).start()

    zero_rim = jnp.zeros((pitch, 128), jnp.float32)
    for slot in range(2):
        for c in range(lanes):
            act[slot, c, pl.ds(0, pitch)] = zero_rim
            act[slot, c, pl.ds((core_h + 1) * pitch, pitch)] = zero_rim
            act[slot, c, pl.ds(pitch + 7, core_h, stride=pitch)] = zero_rim[:core_h]
            act[slot, c, pl.ds(pitch + 8 + core_w, core_h, stride=pitch)] = zero_rim[:core_h]

    x_copy.wait()
    for f in range(frames):
        side = x_ref[f].astype(jnp.float32)
        cols_out[0, f] = side[:, 0, :].astype(jnp.bfloat16)
        cols_out[1, f] = side[:, core_w - 1, :].astype(jnp.bfloat16)
    for_dirs(lambda n: rim_copy(n).start(), True)

    gain = gain_ref[...].reshape(1, channels)
    left, right, up, down = [margin_ref[0, k] for k in range(4)]
    place = slot_ref[group]
    places = [slot_ref[p] for p in partners]
    mine = [jnp.full((1, channels), places[h] == place - 1) for h in (0, 1)]
    theirs = [jnp.full((1, channels), places[h] == places[1 - h] - 1) for h in (0, 1)]

    def choose(hit, a, b):
        return jnp.where(hit, a.astype(jnp.float32), b.astype(jnp.float32))

    not_first = jnp.where(jnp.full((core_h, channels), place > 0), 1.0, 0.0)

    def kept(m):
        m_f = jnp.full((core_h, channels), m, jnp.int32).astype(jnp.float32)
        return (m_f + 1.0) / (m_f + 2.0)

    row_at = lax.broadcasted_iota(jnp.int32, (core_h, channels), 0)
    alpha = [jnp.where(row_at == core_h - down, kept(down), 1.0), None,
             jnp.where(row_at == up - 1, kept(up), 1.0)]
    beta_left = kept(left)
    beta_right = kept(right)

    def put_act(slot, at, v):
        for c in range(lanes):
            act[slot, c, at] = v[:, c * 128:(c + 1) * 128]

    def interior(kind, f, slot, first, last):
        def some_rows(i, carry):
            for h in (0, 1):
                for k in range(2):
                    row = h * half + 2 * i + k
                    if kind:
                        v = choose(mine[h], first_in[f, row, first:last], second_in[f, row, first:last])
                    else:
                        v = x_ref[f, row, first:last]
                    at = pl.multiple_of((row + 1) * pitch + 8 + first, 8)
                    put_act(slot, pl.ds(at, last - first), activate(v, gain))
            return carry
        lax.fori_loop(0, half // 2, some_rows, 0)

    def forward(f, k):
        first, last = pieces[k]
        for h in (0, 1):
            block_pass(1, f, k, h).wait_recv()

        def some_rows(i, carry):
            for h in (0, 1):
                row = h * half + i
                relay[f, row, first:last] = choose(theirs[h], first_in[f, row, first:last],
                                                   x_ref[f, row, first:last]).astype(jnp.bfloat16)
            return carry
        lax.fori_loop(0, half, some_rows, 0, unroll=2)
        for h in (0, 1):
            block_pass(2, f, k, h).start()

    def forward_rim(n):
        rim_pass(1, n).wait_recv()
        hit = theirs[way(n)]
        for f in range(frames):
            rim_at(3, n)[f] = choose(hit, rim_at(1, n)[f], rim_at(0, n)[f]).astype(jnp.bfloat16)
        rim_pass(2, n).start()

    def rims(kind):
        def one(n):
            step_r, step_c = DIRS[n]
            vertical = (core_h + 1) * pitch if step_r > 0 else 0
            for f in range(frames):
                if kind:
                    v = choose(mine[way(n)], rim_at(1, n)[f], rim_at(2, n)[f])
                else:
                    v = rim_at(0, n)[f]
                v = activate(v, gain)
                if step_c == 0:
                    put_act(f, pl.ds(vertical + 8, core_w), v)
                elif step_r == 0:
                    put_act(f, pl.ds(pitch + (8 + core_w if step_c > 0 else 7), core_h, stride=pitch), v)
                else:
                    put_act(f, pl.ds(vertical + (8 + core_w if step_c > 0 else 7), 1), v[0:1] if step_c > 0 else v[7:8])
        for_dirs(one)

    def column(kind, slot, b, p):
        at = pl.ds(b * pitch + 7 + p, core_h, stride=pitch)
        v = jnp.concatenate([act[slot, c, at] for c in range(lanes)], axis=-1)
        if alpha[b] is not None:
            v = v * alpha[b]
        return v * not_first if kind else v

    def spread(kind, slot, first, last):
        def one_col(p, carry):
            for b in range(3):
                z[slot, b, pl.ds(pl.multiple_of(p * core_h, core_h), core_h)] = column(kind, slot, b, p).astype(jnp.bfloat16)
            return carry
        lax.fori_loop(first, last, one_col, 0, unroll=2)

    def spread_left(kind, slot):
        for j in range(M):
            for b in range(3):
                v = column(kind, slot, b, j + 2)
                edge[slot, b, 1, j * core_h:(j + 1) * core_h] = jnp.where(j == left - 1, v * beta_left, v).astype(jnp.bfloat16)

    def spread_right(kind, slot):
        for j in range(M):
            for b in range(3):
                v = column(kind, slot, b, core_w - M + j)
                edge[slot, b, 0, j * core_h:(j + 1) * core_h] = jnp.where(M - j == right, v * beta_right, v).astype(jnp.bfloat16)

    def spread_all(kind, slot):
        spread(kind, slot, 0, core_w + 2)
        spread_left(kind, slot)
        spread_right(kind, slot)

    def windows(slot, j0, j1):
        def rows(ref, first, last):
            return ref[first * core_h:last * core_h]
        out = []
        for b in range(3):
            plain = z.at[slot, b]
            inner = min(j1, core_w - M)
            near = [rows(plain, j0, inner)]
            if j1 > inner:
                near.append(rows(edge.at[slot, b, 0], 0, j1 - inner))
            outer = max(j0, M)
            far = [rows(edge.at[slot, b, 1], j0, M)] if j0 < M else []
            far.append(rows(plain, outer + 2, j1 + 2))
            out += [jnp.concatenate(near, axis=0), rows(plain, j0 + 1, j1 + 1), jnp.concatenate(far, axis=0)]
        return jnp.concatenate(out, axis=-1)

    def product(slot, first, target, at, j0, j1, whole):
        r = jnp.dot(windows(slot, j0, j1), w[:, pl.ds(pl.multiple_of(first * 128, 128), 256)],
                    preferred_element_type=jnp.float32)

        @pl.when(whole)
        def _():
            acc[target, at] += r[:, :128]
        acc[target + 1, at] += r[:, 128:]

    everything = slice(0, core_h * core_w)

    def own_steps(q, carry):
        ahead = jnp.maximum(q - lanes, 0)
        first = jnp.where(q < lanes, 2 * q, ahead)
        target = jnp.where(q < lanes, 2 * q, lanes + ahead)
        product(jnp.where(q < lanes, 0, 1), first, target, everything, 0, core_w, ahead == 0)
        return carry

    def both_steps(n, carry):
        product(1, lanes + 2 * n, 2 * n, everything, 0, core_w, n >= 0)

        @pl.when(n == 0)
        def _():
            forward(0, 1)
        return carry

    def last_steps(j0, j1):
        def step(n, carry):
            product(0, 2 * lanes + n, n, slice(j0 * core_h, j1 * core_h), j0, j1, n == 0)
            return carry
        lax.fori_loop(0, lanes - 1, step, 0)

    bias = bias_ref[...].reshape(1, channels)

    def give(s, first, last):
        def put(i, carry):
            v = jnp.concatenate([acc[s * lanes + c, pl.ds(i + first * core_h, last - first, stride=core_h)]
                                 for c in range(lanes)], axis=-1)
            out_ref[s, i, first:last] = (v + bias).astype(out_ref.dtype)
            return carry
        lax.fori_loop(0, core_h, put, 0, unroll=4)

    def clear(i, carry):
        acc[i] = jnp.zeros(acc.shape[1:], jnp.float32)
        return carry
    lax.fori_loop(0, 2 * lanes, clear, 0)

    interior(0, 0, 0, 0, core_w)
    interior(0, 1, 1, 0, core_w)
    for_dirs(lambda n: rim_copy(opposite(n)).wait_recv())
    for_dirs(lambda n: rim_pass(1, n).start())
    rims(0)
    for f in (0, 1):
        spread_all(0, f)
        forward(1, f)
    for_dirs(forward_rim)
    for h in (0, 1):
        block_pass(1, 0, 1, h).start()
    w_copy(2).wait()
    w_copy(1).wait()
    lax.fori_loop(0, 2 * lanes - 1, own_steps, 0)

    forward(0, 0)
    for k in (0, 1):
        for h in (0, 1):
            block_pass(2, 1, k, h).wait_recv()
    interior(1, 1, 1, 0, core_w)
    for_dirs(lambda n: rim_pass(2, n).wait_recv())
    rims(1)
    spread_all(1, 1)
    w_copy(0).wait()
    lax.fori_loop(0, lanes, both_steps, 0)
    give(1, 0, core_w)

    for h in (0, 1):
        block_pass(2, 0, 0, h).wait_recv()
    interior(1, 0, 0, 0, cut)
    spread(1, 0, 0, cut + 1)
    spread_left(1, 0)
    last_steps(0, cut - 1)
    give(0, 0, cut - 8)
    for h in (0, 1):
        block_pass(2, 0, 1, h).wait_recv()
    interior(1, 0, 0, cut, core_w)
    spread(1, 0, cut + 1, core_w + 2)
    spread_right(1, 0)
    last_steps(cut - 1, core_w)
    give(0, cut - 8, core_w)

    def sent(n):
        rim_copy(n).wait_send()
        for phase in (1, 2):
            rim_pass(phase, n).wait_send()
    for_dirs(sent)
    for phase in (1, 2):
        for f in (1, 0):
            for k in (0, 1):
                for h in (0, 1):
                    block_pass(phase, f, k, h).wait_send()


def local(n_group, n_tile, features, group_slot, margins, norm_gain, kernel, conv_bias):
    x = features[0]
    frames, core_h, core_w, channels = x.shape
    weights = kernel.reshape(3, 9 * channels, channels)
    pitch = core_w + 16
    block = pltpu.VMEM((frames, core_h, core_w, channels), jnp.bfloat16)
    vmem = pl.BlockSpec(memory_space=pltpu.VMEM)
    smem = pl.BlockSpec(memory_space=pltpu.SMEM)
    anywhere = pl.BlockSpec(memory_space=pl.ANY)
    out = pl.pallas_call(
        functools.partial(body, n_group, n_tile),
        out_shape=pltpu.VMEM(x.shape, jnp.bfloat16),
        in_specs=[smem, smem, anywhere, vmem, vmem, anywhere],
        out_specs=vmem,
        scratch_shapes=[
            block, block, block, block,
            pltpu.VMEM((4, 2, frames, core_w, channels), jnp.bfloat16),
            pltpu.VMEM((4, 2, frames, core_h, channels), jnp.bfloat16),
            pltpu.VMEM((4, 2, 2, frames, 8, channels), jnp.bfloat16),
            pltpu.VMEM((2, frames, core_h, channels), jnp.bfloat16),
            pltpu.VMEM((9 * channels, 3 * channels), jnp.bfloat16),
            pltpu.VMEM((2, channels // 128, (core_h + 2) * pitch, 128), jnp.float32),
            pltpu.VMEM((2, 3, (core_w + 2) * core_h, channels), jnp.bfloat16),
            pltpu.VMEM((2, 3, 2, M * core_h, channels), jnp.bfloat16),
            pltpu.VMEM((2 * channels // 128, core_h * core_w, 128), jnp.float32),
            pltpu.SemaphoreType.DMA((3, 8)),
            pltpu.SemaphoreType.DMA((3, 8)),
            pltpu.SemaphoreType.DMA((2, 2, 4)),
            pltpu.SemaphoreType.DMA((2, 2, 4)),
            pltpu.SemaphoreType.DMA((3,)),
            pltpu.SemaphoreType.DMA,
        ],
        compiler_params=pltpu.CompilerParams(collective_id=0, has_side_effects=True, vmem_limit_bytes=60 << 20),
        name="conv",
    )(group_slot, margins, x, norm_gain, conv_bias, weights)
    return out[None]


def solution(mesh):
    n_group = mesh.shape["group"]
    n_tile = mesh.shape["tile"]
    if n_group != 4:
        raise ValueError("group size")
    return jax.shard_map(
        functools.partial(local, n_group, n_tile),
        mesh=mesh,
        in_specs=(
            P(("video", "tile"), "group", None, None, None),
            P(),
            P("tile", None),
            P(),
            P(),
            P(),
        ),
        out_specs=P(("video", "tile"), "group", None, None, None),
        check_vma=False,
    )
```

```python
import functools

import jax
import jax.numpy as jnp
from jax import lax
from jax.experimental import pallas as pl
from jax.experimental.pallas import tpu as pltpu
from jax.sharding import PartitionSpec as P

GRID_R = 2
M = 4
MESH = pl.DeviceIdType.MESH
DIRS = ((-1, 0), (1, 0), (0, -1), (0, 1), (-1, -1), (-1, 1), (1, -1), (1, 1))


def activate(values, gain):
    widened = values.astype(jnp.float32)
    inv_norm = lax.rsqrt(jnp.mean(widened * widened, axis=-1, keepdims=True) + 1e-06)
    half = widened * inv_norm * (0.5 * gain)
    return half + half * jnp.tanh(half)


def body(n_group, n_tile, slot_hbm, margin_hbm, x_hbm, gain_hbm, bias_hbm, w_hbm, out_ref,
         x_ref, first_in, second_in, relay, rows_in, cols_in, corners_in, cols_out, w, act, z, edge, acc,
         send_small, recv_small, send_big, recv_big, w_sem, x_sem,
         slot_ref, margin_ref, gain_ref, bias_ref, small_sem):
    frames, core_h, core_w, channels = x_ref.shape
    grid_cols = n_tile // GRID_R
    lanes = channels // 128
    pitch = core_w + 16
    half = core_h // 2
    cut = core_w - 8
    pieces = ((0, 8), (8, cut), (cut, core_w))
    group = lax.axis_index("group")
    tile = lax.axis_index("tile")
    tile_row = tile // grid_cols
    tile_col = tile % grid_cols
    partners = (group + 1 - 2 * (group % 2), (group + n_group // 2) % n_group)

    def present(step_r, step_c):
        ok = None
        for at, step, most in ((tile_row, step_r, GRID_R), (tile_col, step_c, grid_cols)):
            if step == 0:
                continue
            here = (at > 0) if step < 0 else (at < most - 1)
            ok = here if ok is None else jnp.logical_and(ok, here)
        return ok

    barrier = pltpu.get_barrier_semaphore()
    greeted = jnp.int32(2)
    for peer in partners:
        pl.semaphore_signal(barrier, inc=1, device_id={"group": peer}, device_id_type=MESH)
    for step_r, step_c in DIRS:
        ok = present(step_r, step_c)
        greeted = greeted + ok.astype(jnp.int32)

        @pl.when(ok)
        def _():
            pl.semaphore_signal(barrier, inc=1, device_id={"tile": tile + step_r * grid_cols + step_c},
                                device_id_type=MESH)

    x_copy = pltpu.make_async_copy(x_hbm, x_ref, x_sem)
    x_copy.start()
    small = [pltpu.make_async_copy(a, b, small_sem.at[k]) for k, (a, b) in enumerate(
        ((slot_hbm, slot_ref), (margin_hbm, margin_ref), (gain_hbm, gain_ref), (bias_hbm, bias_ref)))]
    for copy in small:
        copy.start()

    def w_copy(a):
        return pltpu.make_async_copy(w_hbm.at[a], w.at[:, pl.ds((2 - a) * channels, channels)], w_sem.at[a])

    for a in (2, 1, 0):
        w_copy(a).start()

    def rim_at(stage, n):
        step_r, step_c = DIRS[n]
        if step_c == 0:
            return rows_in.at[stage, 1 if step_r > 0 else 0]
        if step_r == 0:
            return cols_in.at[stage, 1 if step_c > 0 else 0]
        return corners_in.at[stage, 1 if step_r > 0 else 0, 1 if step_c > 0 else 0]

    def rim_copy(n):
        step_r, step_c = DIRS[n]
        row = 0 if step_r < 0 else core_h - 1
        if step_c == 0:
            src = x_hbm.at[:, row]
        elif step_r == 0:
            src = cols_out.at[0 if step_c < 0 else 1]
        else:
            src = x_hbm.at[:, row, pl.ds(0 if step_c < 0 else core_w - 8, 8)]
        return pltpu.make_async_remote_copy(
            src_ref=src, dst_ref=rim_at(0, DIRS.index((-step_r, -step_c))),
            send_sem=send_small.at[0, n], recv_sem=recv_small.at[0, n],
            device_id={"tile": tile + step_r * grid_cols + step_c}, device_id_type=MESH)

    def way(n):
        return 0 if DIRS[n][1] == 0 else 1

    def rim_pass(phase, n):
        return pltpu.make_async_remote_copy(
            src_ref=rim_at(0 if phase == 1 else 3, n), dst_ref=rim_at(phase, n),
            send_sem=send_small.at[phase, n], recv_sem=recv_small.at[phase, n],
            device_id={"group": partners[way(n) if phase == 1 else 1 - way(n)]}, device_id_type=MESH)

    def block_pass(phase, f, k, h):
        cols = pl.ds(pieces[k][0], pieces[k][1] - pieces[k][0])
        rows = pl.ds(h * half, half)
        return pltpu.make_async_remote_copy(
            src_ref=(x_hbm if phase == 1 else relay).at[f, rows, cols],
            dst_ref=(first_in if phase == 1 else second_in).at[f, rows, cols],
            send_sem=send_big.at[phase - 1, f, k, h], recv_sem=recv_big.at[phase - 1, f, k, h],
            device_id={"group": partners[h if phase == 1 else 1 - h]}, device_id_type=MESH)

    def for_dirs(act_on, side=None):
        for n, (step_r, step_c) in enumerate(DIRS):
            if side is None or (step_r == 0) == side:
                pl.when(present(step_r, step_c))(functools.partial(act_on, n))

    def opposite(n):
        return DIRS.index((-DIRS[n][0], -DIRS[n][1]))

    pl.semaphore_wait(barrier, greeted)
    for_dirs(lambda n: rim_copy(n).start(), False)
    for f, k in ((1, 0), (1, 1), (1, 2), (0, 0)):
        for h in (0, 1):
            block_pass(1, f, k, h).start()

    zero_rim = jnp.zeros((pitch, 128), jnp.float32)
    for slot in range(2):
        for c in range(lanes):
            act[slot, c, pl.ds(0, pitch)] = zero_rim
            act[slot, c, pl.ds((core_h + 1) * pitch, pitch)] = zero_rim
            act[slot, c, pl.ds(pitch + 7, core_h, stride=pitch)] = zero_rim[:core_h]
            act[slot, c, pl.ds(pitch + 8 + core_w, core_h, stride=pitch)] = zero_rim[:core_h]

    x_copy.wait()
    for f in range(frames):
        side = x_ref[f].astype(jnp.float32)
        cols_out[0, f] = side[:, 0, :].astype(jnp.bfloat16)
        cols_out[1, f] = side[:, core_w - 1, :].astype(jnp.bfloat16)
    for_dirs(lambda n: rim_copy(n).start(), True)

    for copy in small:
        copy.wait()
    gain = gain_ref[...].reshape(1, channels)
    left, right, up, down = [margin_ref[0, k] for k in range(4)]
    place = slot_ref[group]
    places = [slot_ref[p] for p in partners]
    mine = [jnp.full((1, channels), places[h] == place - 1) for h in (0, 1)]
    theirs = [jnp.full((1, channels), places[h] == places[1 - h] - 1) for h in (0, 1)]

    def choose(hit, a, b):
        return jnp.where(hit, a.astype(jnp.float32), b.astype(jnp.float32))

    not_first = jnp.where(jnp.full((core_h, channels), place > 0), 1.0, 0.0)

    def kept(m):
        m_f = jnp.full((core_h, channels), m, jnp.int32).astype(jnp.float32)
        return (m_f + 1.0) / (m_f + 2.0)

    row_at = lax.broadcasted_iota(jnp.int32, (core_h, channels), 0)
    alpha = [jnp.where(row_at == core_h - down, kept(down), 1.0), None,
             jnp.where(row_at == up - 1, kept(up), 1.0)]
    beta_left = kept(left)
    beta_right = kept(right)

    def put_act(slot, at, v):
        for c in range(lanes):
            act[slot, c, at] = v[:, c * 128:(c + 1) * 128]

    def interior(kind, f, slot, first, last):
        def some_rows(i, carry):
            for h in (0, 1):
                for k in range(4):
                    row = h * half + 4 * i + k
                    if kind:
                        v = choose(mine[h], first_in[f, row, first:last], second_in[f, row, first:last])
                    else:
                        v = x_ref[f, row, first:last]
                    at = pl.multiple_of((row + 1) * pitch + 8 + first, 8)
                    put_act(slot, pl.ds(at, last - first), activate(v, gain))
            return carry
        lax.fori_loop(0, half // 4, some_rows, 0)

    def forward(f, k):
        first, last = pieces[k]
        for h in (0, 1):
            block_pass(1, f, k, h).wait_recv()

        def some_rows(i, carry):
            for h in (0, 1):
                row = h * half + i
                relay[f, row, first:last] = choose(theirs[h], first_in[f, row, first:last],
                                                   x_ref[f, row, first:last]).astype(jnp.bfloat16)
            return carry
        lax.fori_loop(0, half, some_rows, 0, unroll=2)
        for h in (0, 1):
            block_pass(2, f, k, h).start()

    def forward_rim(n):
        rim_pass(1, n).wait_recv()
        hit = theirs[way(n)]
        for f in range(frames):
            rim_at(3, n)[f] = choose(hit, rim_at(1, n)[f], rim_at(0, n)[f]).astype(jnp.bfloat16)
        rim_pass(2, n).start()

    def rims(kind):
        def one(n):
            step_r, step_c = DIRS[n]
            vertical = (core_h + 1) * pitch if step_r > 0 else 0
            for f in range(frames):
                if kind:
                    v = choose(mine[way(n)], rim_at(1, n)[f], rim_at(2, n)[f])
                else:
                    v = rim_at(0, n)[f]
                v = activate(v, gain)
                if step_c == 0:
                    put_act(f, pl.ds(vertical + 8, core_w), v)
                elif step_r == 0:
                    put_act(f, pl.ds(pitch + (8 + core_w if step_c > 0 else 7), core_h, stride=pitch), v)
                else:
                    put_act(f, pl.ds(vertical + (8 + core_w if step_c > 0 else 7), 1), v[0:1] if step_c > 0 else v[7:8])
        for_dirs(one)

    def column(kind, slot, b, p):
        at = pl.ds(b * pitch + 7 + p, core_h, stride=pitch)
        v = jnp.concatenate([act[slot, c, at] for c in range(lanes)], axis=-1)
        if alpha[b] is not None:
            v = v * alpha[b]
        return v * not_first if kind else v

    def spread(kind, slot, first, last):
        def one_col(p, carry):
            for b in range(3):
                z[slot, b, pl.ds(pl.multiple_of(p * core_h, core_h), core_h)] = column(kind, slot, b, p).astype(jnp.bfloat16)
            return carry
        lax.fori_loop(first, last, one_col, 0, unroll=2)

    def spread_left(kind, slot):
        for j in range(M):
            for b in range(3):
                v = column(kind, slot, b, j + 2)
                edge[slot, b, 1, j * core_h:(j + 1) * core_h] = jnp.where(j == left - 1, v * beta_left, v).astype(jnp.bfloat16)

    def spread_right(kind, slot):
        for j in range(M):
            for b in range(3):
                v = column(kind, slot, b, core_w - M + j)
                edge[slot, b, 0, j * core_h:(j + 1) * core_h] = jnp.where(M - j == right, v * beta_right, v).astype(jnp.bfloat16)

    def spread_all(kind, slot):
        spread(kind, slot, 0, core_w + 2)
        spread_left(kind, slot)
        spread_right(kind, slot)

    def windows(slot, j0, j1):
        def rows(ref, first, last):
            return ref[first * core_h:last * core_h]
        out = []
        for b in range(3):
            plain = z.at[slot, b]
            inner = min(j1, core_w - M)
            near = [rows(plain, j0, inner)]
            if j1 > inner:
                near.append(rows(edge.at[slot, b, 0], 0, j1 - inner))
            outer = max(j0, M)
            far = [rows(edge.at[slot, b, 1], j0, M)] if j0 < M else []
            far.append(rows(plain, outer + 2, j1 + 2))
            out += [jnp.concatenate(near, axis=0), rows(plain, j0 + 1, j1 + 1), jnp.concatenate(far, axis=0)]
        return jnp.concatenate(out, axis=-1)

    def product(slot, first, target, at, j0, j1, whole):
        r = jnp.dot(windows(slot, j0, j1), w[:, pl.ds(pl.multiple_of(first * 128, 128), 256)],
                    preferred_element_type=jnp.float32)

        def left_part():
            acc[target, at] += r[:, :128]
        if whole is None:
            left_part()
        else:
            pl.when(whole)(left_part)
        acc[target + 1, at] += r[:, 128:]

    everything = slice(0, core_h * core_w)

    def at_step(n, turn, act_on):
        pl.when(n == turn)(act_on)

    def forward_next():
        for k in range(3):
            forward(1, k)

    def send_last():
        for_dirs(forward_rim)
        for k in (1, 2):
            for h in (0, 1):
                block_pass(1, 0, k, h).start()
        forward(0, 0)

    def forward_last():
        for k in (1, 2):
            forward(0, k)

    def own_both(n, carry):
        product(0, 2 * n, 2 * n, everything, 0, core_w, None)
        at_step(n, 0, send_last)
        return carry

    def own_single(n, carry):
        product(1, n, lanes + n, everything, 0, core_w, n == 0)
        return carry

    def both_steps(n, carry):
        product(1, lanes + 2 * n, 2 * n, everything, 0, core_w, None)
        at_step(n, 0, forward_last)
        return carry

    def last_steps(j0, j1):
        def step(n, carry):
            product(0, 2 * lanes + n, n, slice(j0 * core_h, j1 * core_h), j0, j1, n == 0)
            return carry
        lax.fori_loop(0, lanes - 1, step, 0)

    bias = bias_ref[...].reshape(1, channels)

    def give(s, first, last):
        def put(i, carry):
            v = jnp.concatenate([acc[s * lanes + c, pl.ds(i + first * core_h, last - first, stride=core_h)]
                                 for c in range(lanes)], axis=-1)
            out_ref[s, i, first:last] = (v + bias).astype(out_ref.dtype)
            return carry
        lax.fori_loop(0, core_h, put, 0, unroll=4)

    def clear(i, carry):
        acc[i] = jnp.zeros(acc.shape[1:], jnp.float32)
        return carry
    lax.fori_loop(0, 2 * lanes, clear, 0)

    interior(0, 0, 0, 0, core_w)
    interior(0, 1, 1, 0, core_w)
    for_dirs(lambda n: rim_copy(opposite(n)).wait_recv())
    for_dirs(lambda n: rim_pass(1, n).start())
    rims(0)
    for f in (0, 1):
        spread_all(0, f)
    forward_next()
    w_copy(2).wait()
    w_copy(1).wait()
    lax.fori_loop(0, lanes, own_both, 0)
    lax.fori_loop(0, lanes - 1, own_single, 0)

    for k, (first, last) in enumerate(pieces):
        for h in (0, 1):
            block_pass(2, 1, k, h).wait_recv()
        interior(1, 1, 1, first, last)
    for_dirs(lambda n: rim_pass(2, n).wait_recv())
    rims(1)
    spread_all(1, 1)
    w_copy(0).wait()
    lax.fori_loop(0, lanes, both_steps, 0)
    give(1, 0, core_w)

    for k in (0, 1):
        for h in (0, 1):
            block_pass(2, 0, k, h).wait_recv()
    interior(1, 0, 0, 0, cut)
    spread(1, 0, 0, cut + 1)
    spread_left(1, 0)
    last_steps(0, cut - 1)
    for h in (0, 1):
        block_pass(2, 0, 2, h).wait_recv()
    interior(1, 0, 0, cut, core_w)
    spread(1, 0, cut + 1, core_w + 2)
    spread_right(1, 0)
    last_steps(cut - 1, core_w)
    give(0, 0, core_w)

    def sent(n):
        rim_copy(n).wait_send()
        for phase in (1, 2):
            rim_pass(phase, n).wait_send()
    for_dirs(sent)
    for phase in (1, 2):
        for f in (1, 0):
            for k in range(3):
                for h in (0, 1):
                    block_pass(phase, f, k, h).wait_send()


def local(n_group, n_tile, features, group_slot, margins, norm_gain, kernel, conv_bias):
    x = features[0]
    frames, core_h, core_w, channels = x.shape
    weights = kernel.reshape(3, 9 * channels, channels)
    pitch = core_w + 16
    block = pltpu.VMEM((frames, core_h, core_w, channels), jnp.bfloat16)
    vmem = pl.BlockSpec(memory_space=pltpu.VMEM)
    anywhere = pl.BlockSpec(memory_space=pl.ANY)
    out = pl.pallas_call(
        functools.partial(body, n_group, n_tile),
        out_shape=pltpu.VMEM(x.shape, jnp.bfloat16),
        in_specs=[anywhere] * 6,
        out_specs=vmem,
        scratch_shapes=[
            block, block, block, block,
            pltpu.VMEM((4, 2, frames, core_w, channels), jnp.bfloat16),
            pltpu.VMEM((4, 2, frames, core_h, channels), jnp.bfloat16),
            pltpu.VMEM((4, 2, 2, frames, 8, channels), jnp.bfloat16),
            pltpu.VMEM((2, frames, core_h, channels), jnp.bfloat16),
            pltpu.VMEM((9 * channels, 3 * channels), jnp.bfloat16),
            pltpu.VMEM((2, channels // 128, (core_h + 2) * pitch, 128), jnp.float32),
            pltpu.VMEM((2, 3, (core_w + 2) * core_h, channels), jnp.bfloat16),
            pltpu.VMEM((2, 3, 2, M * core_h, channels), jnp.bfloat16),
            pltpu.VMEM((2 * channels // 128, core_h * core_w, 128), jnp.float32),
            pltpu.SemaphoreType.DMA((3, 8)),
            pltpu.SemaphoreType.DMA((3, 8)),
            pltpu.SemaphoreType.DMA((2, 2, 3, 2)),
            pltpu.SemaphoreType.DMA((2, 2, 3, 2)),
            pltpu.SemaphoreType.DMA((3,)),
            pltpu.SemaphoreType.DMA,
            pltpu.SMEM(group_slot.shape, jnp.int32),
            pltpu.SMEM(margins.shape, jnp.int32),
            pltpu.VMEM(norm_gain.shape, jnp.float32),
            pltpu.VMEM(conv_bias.shape, jnp.float32),
            pltpu.SemaphoreType.DMA((4,)),
        ],
        compiler_params=pltpu.CompilerParams(collective_id=0, has_side_effects=True, vmem_limit_bytes=60 << 20),
        name="conv",
    )(group_slot, margins, x, norm_gain, conv_bias, weights)
    return out[None]


def solution(mesh):
    n_group = mesh.shape["group"]
    n_tile = mesh.shape["tile"]
    if n_group != 4:
        raise ValueError("group size")
    return jax.shard_map(
        functools.partial(local, n_group, n_tile),
        mesh=mesh,
        in_specs=(
            P(("video", "tile"), "group", None, None, None),
            P(),
            P("tile", None),
            P(),
            P(),
            P(),
        ),
        out_specs=P(("video", "tile"), "group", None, None, None),
        check_vma=False,
    )
```

```python
import functools

import jax
import jax.numpy as jnp
from jax import lax
from jax.experimental import pallas as pl
from jax.experimental.pallas import tpu as pltpu
from jax.sharding import PartitionSpec as P

GRID_R = 2
M = 4
MESH = pl.DeviceIdType.MESH
DIRS = ((-1, 0), (1, 0), (0, -1), (0, 1), (-1, -1), (-1, 1), (1, -1), (1, 1))


def activate(values, gain):
    widened = values.astype(jnp.float32)
    inv_norm = lax.rsqrt(jnp.mean(widened * widened, axis=-1, keepdims=True) + 1e-06)
    half = widened * inv_norm * (0.5 * gain)
    return half + half * jnp.tanh(half)


def body(n_group, n_tile, slot_hbm, margin_hbm, x_hbm, gain_hbm, bias_hbm, w_hbm, out_ref,
         x_ref, first_in, second_in, relay, rows_in, cols_in, corners_in, cols_out, w, act, z, edge, acc,
         send_small, recv_small, send_big, recv_big, w_sem, x_sem,
         slot_ref, margin_ref, gain_ref, bias_ref, small_sem):
    frames, core_h, core_w, channels = x_ref.shape
    grid_cols = n_tile // GRID_R
    lanes = channels // 128
    pitch = core_w + 16
    half = core_h // 2
    cut = core_w - 8
    pieces = ((0, 8), (8, cut), (cut, core_w))
    group = lax.axis_index("group")
    tile = lax.axis_index("tile")
    tile_row = tile // grid_cols
    tile_col = tile % grid_cols
    partners = (group + 1 - 2 * (group % 2), (group + n_group // 2) % n_group)

    def present(step_r, step_c):
        ok = None
        for at, step, most in ((tile_row, step_r, GRID_R), (tile_col, step_c, grid_cols)):
            if step == 0:
                continue
            here = (at > 0) if step < 0 else (at < most - 1)
            ok = here if ok is None else jnp.logical_and(ok, here)
        return ok

    barrier = pltpu.get_barrier_semaphore()
    greeted = jnp.int32(2)
    for peer in partners:
        pl.semaphore_signal(barrier, inc=1, device_id={"group": peer}, device_id_type=MESH)
    for step_r, step_c in DIRS:
        ok = present(step_r, step_c)
        greeted = greeted + ok.astype(jnp.int32)

        @pl.when(ok)
        def _():
            pl.semaphore_signal(barrier, inc=1, device_id={"tile": tile + step_r * grid_cols + step_c},
                                device_id_type=MESH)

    x_copy = pltpu.make_async_copy(x_hbm, x_ref, x_sem)
    x_copy.start()
    small = [pltpu.make_async_copy(a, b, small_sem.at[k]) for k, (a, b) in enumerate(
        ((slot_hbm, slot_ref), (margin_hbm, margin_ref), (gain_hbm, gain_ref), (bias_hbm, bias_ref)))]
    for copy in small:
        copy.start()

    def w_copy(a):
        return pltpu.make_async_copy(w_hbm.at[a], w.at[:, pl.ds((2 - a) * channels, channels)], w_sem.at[a])

    for a in (2, 1, 0):
        w_copy(a).start()

    def rim_at(stage, n):
        step_r, step_c = DIRS[n]
        if step_c == 0:
            return rows_in.at[stage, 1 if step_r > 0 else 0]
        if step_r == 0:
            return cols_in.at[stage, 1 if step_c > 0 else 0]
        return corners_in.at[stage, 1 if step_r > 0 else 0, 1 if step_c > 0 else 0]

    def rim_copy(n):
        step_r, step_c = DIRS[n]
        row = 0 if step_r < 0 else core_h - 1
        if step_c == 0:
            src = x_hbm.at[:, row]
        elif step_r == 0:
            src = cols_out.at[0 if step_c < 0 else 1]
        else:
            src = x_hbm.at[:, row, pl.ds(0 if step_c < 0 else core_w - 8, 8)]
        return pltpu.make_async_remote_copy(
            src_ref=src, dst_ref=rim_at(0, DIRS.index((-step_r, -step_c))),
            send_sem=send_small.at[0, n], recv_sem=recv_small.at[0, n],
            device_id={"tile": tile + step_r * grid_cols + step_c}, device_id_type=MESH)

    def way(n):
        return 0 if DIRS[n][1] == 0 else 1

    def rim_pass(phase, n):
        return pltpu.make_async_remote_copy(
            src_ref=rim_at(0 if phase == 1 else 3, n), dst_ref=rim_at(phase, n),
            send_sem=send_small.at[phase, n], recv_sem=recv_small.at[phase, n],
            device_id={"group": partners[way(n) if phase == 1 else 1 - way(n)]}, device_id_type=MESH)

    def block_pass(phase, f, k, h):
        cols = pl.ds(pieces[k][0], pieces[k][1] - pieces[k][0])
        rows = pl.ds(h * half, half)
        return pltpu.make_async_remote_copy(
            src_ref=(x_hbm if phase == 1 else relay).at[f, rows, cols],
            dst_ref=(first_in if phase == 1 else second_in).at[f, rows, cols],
            send_sem=send_big.at[phase - 1, f, k, h], recv_sem=recv_big.at[phase - 1, f, k, h],
            device_id={"group": partners[h if phase == 1 else 1 - h]}, device_id_type=MESH)

    def for_dirs(act_on, side=None):
        for n, (step_r, step_c) in enumerate(DIRS):
            if side is None or (step_r == 0) == side:
                pl.when(present(step_r, step_c))(functools.partial(act_on, n))

    def opposite(n):
        return DIRS.index((-DIRS[n][0], -DIRS[n][1]))

    pl.semaphore_wait(barrier, greeted)
    for_dirs(lambda n: rim_copy(n).start(), False)
    for f, k in ((1, 0), (1, 1), (1, 2), (0, 0)):
        for h in (0, 1):
            block_pass(1, f, k, h).start()

    zero_rim = jnp.zeros((pitch, 128), jnp.float32)
    for slot in range(2):
        for c in range(lanes):
            act[slot, c, pl.ds(0, pitch)] = zero_rim
            act[slot, c, pl.ds((core_h + 1) * pitch, pitch)] = zero_rim
            act[slot, c, pl.ds(pitch + 7, core_h, stride=pitch)] = zero_rim[:core_h]
            act[slot, c, pl.ds(pitch + 8 + core_w, core_h, stride=pitch)] = zero_rim[:core_h]

    x_copy.wait()
    for f in range(frames):
        side = x_ref[f].astype(jnp.float32)
        cols_out[0, f] = side[:, 0, :].astype(jnp.bfloat16)
        cols_out[1, f] = side[:, core_w - 1, :].astype(jnp.bfloat16)
    for_dirs(lambda n: rim_copy(n).start(), True)

    for copy in small:
        copy.wait()
    gain = gain_ref[...].reshape(1, channels)
    left, right, up, down = [margin_ref[0, k] for k in range(4)]
    place = slot_ref[group]
    places = [slot_ref[p] for p in partners]
    mine = [jnp.full((1, channels), places[h] == place - 1) for h in (0, 1)]
    theirs = [jnp.full((1, channels), places[h] == places[1 - h] - 1) for h in (0, 1)]

    def choose(hit, a, b):
        return jnp.where(hit, a.astype(jnp.float32), b.astype(jnp.float32))

    not_first = jnp.where(jnp.full((core_h, channels), place > 0), 1.0, 0.0)

    def kept(m):
        m_f = jnp.full((core_h, channels), m, jnp.int32).astype(jnp.float32)
        return (m_f + 1.0) / (m_f + 2.0)

    row_at = lax.broadcasted_iota(jnp.int32, (core_h, channels), 0)
    alpha = [jnp.where(row_at == core_h - down, kept(down), 1.0), None,
             jnp.where(row_at == up - 1, kept(up), 1.0)]
    beta_left = kept(left)
    beta_right = kept(right)

    def put_act(slot, at, v):
        for c in range(lanes):
            act[slot, c, at] = v[:, c * 128:(c + 1) * 128]

    def interior(kind, f, slot, first, last):
        many = half // 2 if last - first > 8 else half

        def some_rows(i, carry):
            for h in (0, 1):
                for k in range(many):
                    row = h * half + many * i + k
                    if kind:
                        v = choose(mine[h], first_in[f, row, first:last], second_in[f, row, first:last])
                    else:
                        v = x_ref[f, row, first:last]
                    at = pl.multiple_of((row + 1) * pitch + 8 + first, 8)
                    put_act(slot, pl.ds(at, last - first), activate(v, gain))
            return carry
        lax.fori_loop(0, half // many, some_rows, 0)

    def forward(f, k):
        first, last = pieces[k]
        for h in (0, 1):
            block_pass(1, f, k, h).wait_recv()

        def some_rows(i, carry):
            for h in (0, 1):
                row = h * half + i
                relay[f, row, first:last] = choose(theirs[h], first_in[f, row, first:last],
                                                   x_ref[f, row, first:last]).astype(jnp.bfloat16)
            return carry
        lax.fori_loop(0, half, some_rows, 0, unroll=2)
        for h in (0, 1):
            block_pass(2, f, k, h).start()

    def forward_rim(n):
        rim_pass(1, n).wait_recv()
        hit = theirs[way(n)]
        for f in range(frames):
            rim_at(3, n)[f] = choose(hit, rim_at(1, n)[f], rim_at(0, n)[f]).astype(jnp.bfloat16)
        rim_pass(2, n).start()

    def rims(kind):
        def one(n):
            step_r, step_c = DIRS[n]
            vertical = (core_h + 1) * pitch if step_r > 0 else 0
            for f in range(frames):
                if kind:
                    v = choose(mine[way(n)], rim_at(1, n)[f], rim_at(2, n)[f])
                else:
                    v = rim_at(0, n)[f]
                v = activate(v, gain)
                if step_c == 0:
                    put_act(f, pl.ds(vertical + 8, core_w), v)
                elif step_r == 0:
                    put_act(f, pl.ds(pitch + (8 + core_w if step_c > 0 else 7), core_h, stride=pitch), v)
                else:
                    put_act(f, pl.ds(vertical + (8 + core_w if step_c > 0 else 7), 1), v[0:1] if step_c > 0 else v[7:8])
        for_dirs(one)

    def column(kind, slot, b, p):
        at = pl.ds(b * pitch + 7 + p, core_h, stride=pitch)
        v = jnp.concatenate([act[slot, c, at] for c in range(lanes)], axis=-1)
        if alpha[b] is not None:
            v = v * alpha[b]
        return v * not_first if kind else v

    def spread(kind, slot, first, last):
        def one_col(p, carry):
            for b in range(3):
                z[slot, b, pl.ds(pl.multiple_of(p * core_h, core_h), core_h)] = column(kind, slot, b, p).astype(jnp.bfloat16)
            return carry
        lax.fori_loop(first, last, one_col, 0, unroll=3)

    def spread_left(kind, slot):
        for j in range(M):
            for b in range(3):
                v = column(kind, slot, b, j + 2)
                edge[slot, b, 1, j * core_h:(j + 1) * core_h] = jnp.where(j == left - 1, v * beta_left, v).astype(jnp.bfloat16)

    def spread_right(kind, slot):
        for j in range(M):
            for b in range(3):
                v = column(kind, slot, b, core_w - M + j)
                edge[slot, b, 0, j * core_h:(j + 1) * core_h] = jnp.where(M - j == right, v * beta_right, v).astype(jnp.bfloat16)

    def spread_all(kind, slot):
        spread(kind, slot, 0, core_w + 2)
        spread_left(kind, slot)
        spread_right(kind, slot)

    def windows(slot, j0, j1):
        def rows(ref, first, last):
            return ref[first * core_h:last * core_h]
        out = []
        for b in range(3):
            plain = z.at[slot, b]
            inner = min(j1, core_w - M)
            near = [rows(plain, j0, inner)]
            if j1 > inner:
                near.append(rows(edge.at[slot, b, 0], 0, j1 - inner))
            outer = max(j0, M)
            far = [rows(edge.at[slot, b, 1], j0, M)] if j0 < M else []
            far.append(rows(plain, outer + 2, j1 + 2))
            out += [jnp.concatenate(near, axis=0), rows(plain, j0 + 1, j1 + 1), jnp.concatenate(far, axis=0)]
        return jnp.concatenate(out, axis=-1)

    def product(slot, first, target, at, j0, j1, whole):
        r = jnp.dot(windows(slot, j0, j1), w[:, pl.ds(pl.multiple_of(first * 128, 128), 256)],
                    preferred_element_type=jnp.float32)

        def left_part():
            acc[target, at] += r[:, :128]
        if whole is None:
            left_part()
        else:
            pl.when(whole)(left_part)
        acc[target + 1, at] += r[:, 128:]

    everything = slice(0, core_h * core_w)

    def at_step(n, turn, act_on):
        pl.when(n == turn)(act_on)

    def forward_next():
        for k in range(3):
            forward(1, k)

    def send_last():
        for_dirs(forward_rim)
        for k in (1, 2):
            for h in (0, 1):
                block_pass(1, 0, k, h).start()
        forward(0, 0)

    def forward_last():
        for k in (1, 2):
            forward(0, k)

    def own_both(n, carry):
        product(0, 2 * n, 2 * n, everything, 0, core_w, None)
        at_step(n, 0, send_last)
        return carry

    def own_single(n, carry):
        product(1, n, lanes + n, everything, 0, core_w, n == 0)
        return carry

    def both_steps(n, carry):
        product(1, lanes + 2 * n, 2 * n, everything, 0, core_w, None)
        at_step(n, 0, forward_last)
        return carry

    def static_product(slot, first, target, many, j0, j1):
        r = jnp.dot(windows(slot, j0, j1), w[:, first * 128:(first + many) * 128],
                    preferred_element_type=jnp.float32)
        for c in range(many):
            acc[target + c, j0 * core_h:j1 * core_h] += r[:, c * 128:(c + 1) * 128]

    bias = bias_ref[...].reshape(1, channels)

    def give(s, first, last):
        def put(i, carry):
            v = jnp.concatenate([acc[s * lanes + c, pl.ds(i + first * core_h, last - first, stride=core_h)]
                                 for c in range(lanes)], axis=-1)
            out_ref[s, i, first:last] = (v + bias).astype(out_ref.dtype)
            return carry
        lax.fori_loop(0, core_h, put, 0, unroll=8)

    def clear(i, carry):
        acc[i] = jnp.zeros(acc.shape[1:], jnp.float32)
        return carry
    lax.fori_loop(0, 2 * lanes, clear, 0)

    interior(0, 0, 0, 0, core_w)
    interior(0, 1, 1, 0, core_w)
    for_dirs(lambda n: rim_copy(opposite(n)).wait_recv())
    for_dirs(lambda n: rim_pass(1, n).start())
    rims(0)
    for f in (0, 1):
        spread_all(0, f)
    forward_next()
    w_copy(2).wait()
    w_copy(1).wait()
    lax.fori_loop(0, lanes, own_both, 0)
    lax.fori_loop(0, lanes - 1, own_single, 0)

    for k, (first, last) in enumerate(pieces):
        for h in (0, 1):
            block_pass(2, 1, k, h).wait_recv()
        interior(1, 1, 1, first, last)
    for_dirs(lambda n: rim_pass(2, n).wait_recv())
    rims(1)
    spread_all(1, 1)
    w_copy(0).wait()
    lax.fori_loop(0, lanes, both_steps, 0)
    give(1, 0, core_w)

    def sent(n):
        rim_copy(n).wait_send()
        for phase in (1, 2):
            rim_pass(phase, n).wait_send()
    for_dirs(sent)
    for phase, f in ((1, 1), (2, 1), (1, 0)):
        for k in range(3):
            for h in (0, 1):
                block_pass(phase, f, k, h).wait_send()

    for k in (0, 1):
        for h in (0, 1):
            block_pass(2, 0, k, h).wait_recv()
        interior(1, 0, 0, *pieces[k])
    spread(1, 0, 0, cut + 1)
    spread_left(1, 0)
    for h in (0, 1):
        block_pass(2, 0, 2, h).wait_recv()
    interior(1, 0, 0, cut, core_w)
    spread(1, 0, cut + 1, core_w + 2)
    spread_right(1, 0)
    static_product(0, 2 * lanes, 0, lanes, 0, core_w)
    give(0, 0, core_w)
    for k in range(3):
        for h in (0, 1):
            block_pass(2, 0, k, h).wait_send()


def local(n_group, n_tile, features, group_slot, margins, norm_gain, kernel, conv_bias):
    x = features[0]
    frames, core_h, core_w, channels = x.shape
    weights = kernel.reshape(3, 9 * channels, channels)
    pitch = core_w + 16
    block = pltpu.VMEM((frames, core_h, core_w, channels), jnp.bfloat16)
    vmem = pl.BlockSpec(memory_space=pltpu.VMEM)
    anywhere = pl.BlockSpec(memory_space=pl.ANY)
    out = pl.pallas_call(
        functools.partial(body, n_group, n_tile),
        out_shape=pltpu.VMEM(x.shape, jnp.bfloat16),
        in_specs=[anywhere] * 6,
        out_specs=vmem,
        scratch_shapes=[
            block, block, block, block,
            pltpu.VMEM((4, 2, frames, core_w, channels), jnp.bfloat16),
            pltpu.VMEM((4, 2, frames, core_h, channels), jnp.bfloat16),
            pltpu.VMEM((4, 2, 2, frames, 8, channels), jnp.bfloat16),
            pltpu.VMEM((2, frames, core_h, channels), jnp.bfloat16),
            pltpu.VMEM((9 * channels, 3 * channels), jnp.bfloat16),
            pltpu.VMEM((2, channels // 128, (core_h + 2) * pitch, 128), jnp.float32),
            pltpu.VMEM((2, 3, (core_w + 2) * core_h, channels), jnp.bfloat16),
            pltpu.VMEM((2, 3, 2, M * core_h, channels), jnp.bfloat16),
            pltpu.VMEM((2 * channels // 128, core_h * core_w, 128), jnp.float32),
            pltpu.SemaphoreType.DMA((3, 8)),
            pltpu.SemaphoreType.DMA((3, 8)),
            pltpu.SemaphoreType.DMA((2, 2, 3, 2)),
            pltpu.SemaphoreType.DMA((2, 2, 3, 2)),
            pltpu.SemaphoreType.DMA((3,)),
            pltpu.SemaphoreType.DMA,
            pltpu.SMEM(group_slot.shape, jnp.int32),
            pltpu.SMEM(margins.shape, jnp.int32),
            pltpu.VMEM(norm_gain.shape, jnp.float32),
            pltpu.VMEM(conv_bias.shape, jnp.float32),
            pltpu.SemaphoreType.DMA((4,)),
        ],
        compiler_params=pltpu.CompilerParams(collective_id=0, has_side_effects=True, vmem_limit_bytes=60 << 20),
        name="conv",
    )(group_slot, margins, x, norm_gain, conv_bias, weights)
    return out[None]


def solution(mesh):
    n_group = mesh.shape["group"]
    n_tile = mesh.shape["tile"]
    if n_group != 4:
        raise ValueError("group size")
    return jax.shard_map(
        functools.partial(local, n_group, n_tile),
        mesh=mesh,
        in_specs=(
            P(("video", "tile"), "group", None, None, None),
            P(),
            P("tile", None),
            P(),
            P(),
            P(),
        ),
        out_specs=P(("video", "tile"), "group", None, None, None),
        check_vma=False,
    )
```

```python
import functools

import jax
import jax.numpy as jnp
from jax import lax
from jax.experimental import pallas as pl
from jax.experimental.pallas import tpu as pltpu
from jax.sharding import PartitionSpec as P

GRID_R = 2
M = 4
MESH = pl.DeviceIdType.MESH
DIRS = ((-1, 0), (1, 0), (0, -1), (0, 1), (-1, -1), (-1, 1), (1, -1), (1, 1))


def activate(values, gain):
    widened = values.astype(jnp.float32)
    inv_norm = lax.rsqrt(jnp.mean(widened * widened, axis=-1, keepdims=True) + 1e-06)
    half = widened * inv_norm * (0.5 * gain)
    return half + half * jnp.tanh(half)


def body(n_group, n_tile, slot_hbm, margin_hbm, x_hbm, gain_hbm, bias_hbm, w_hbm, out_ref,
         x_ref, first_in, second_in, relay, rows_in, cols_in, corners_in, cols_out, w, act, z, edge, acc,
         send_small, recv_small, send_big, recv_big, w_sem, x_sem,
         slot_ref, margin_ref, gain_ref, bias_ref, small_sem):
    frames, core_h, core_w, channels = x_ref.shape
    grid_cols = n_tile // GRID_R
    lanes = channels // 128
    pitch = core_w + 16
    half = core_h // 2
    cut = core_w - 8
    pieces = ((0, 8), (8, cut), (cut, core_w))
    group = lax.axis_index("group")
    tile = lax.axis_index("tile")
    tile_row = tile // grid_cols
    tile_col = tile % grid_cols
    partners = (group + 1 - 2 * (group % 2), (group + n_group // 2) % n_group)

    def present(step_r, step_c):
        ok = None
        for at, step, most in ((tile_row, step_r, GRID_R), (tile_col, step_c, grid_cols)):
            if step == 0:
                continue
            here = (at > 0) if step < 0 else (at < most - 1)
            ok = here if ok is None else jnp.logical_and(ok, here)
        return ok

    barrier = pltpu.get_barrier_semaphore()
    greeted = jnp.int32(2)
    for peer in partners:
        pl.semaphore_signal(barrier, inc=1, device_id={"group": peer}, device_id_type=MESH)
    for step_r, step_c in DIRS:
        ok = present(step_r, step_c)
        greeted = greeted + ok.astype(jnp.int32)

        @pl.when(ok)
        def _():
            pl.semaphore_signal(barrier, inc=1, device_id={"tile": tile + step_r * grid_cols + step_c},
                                device_id_type=MESH)

    x_copy = pltpu.make_async_copy(x_hbm, x_ref, x_sem)
    x_copy.start()
    small = [pltpu.make_async_copy(a, b, small_sem.at[k]) for k, (a, b) in enumerate(
        ((slot_hbm, slot_ref), (margin_hbm, margin_ref), (gain_hbm, gain_ref), (bias_hbm, bias_ref)))]
    for copy in small:
        copy.start()

    def w_copy(a):
        return pltpu.make_async_copy(w_hbm.at[a], w.at[:, pl.ds((2 - a) * channels, channels)], w_sem.at[a])

    for a in (2, 1, 0):
        w_copy(a).start()

    def rim_at(stage, n):
        step_r, step_c = DIRS[n]
        if step_c == 0:
            return rows_in.at[stage, 1 if step_r > 0 else 0]
        if step_r == 0:
            return cols_in.at[stage, 1 if step_c > 0 else 0]
        return corners_in.at[stage, 1 if step_r > 0 else 0, 1 if step_c > 0 else 0]

    def rim_copy(n):
        step_r, step_c = DIRS[n]
        row = 0 if step_r < 0 else core_h - 1
        if step_c == 0:
            src = x_hbm.at[:, row]
        elif step_r == 0:
            src = cols_out.at[0 if step_c < 0 else 1]
        else:
            src = x_hbm.at[:, row, pl.ds(0 if step_c < 0 else core_w - 8, 8)]
        return pltpu.make_async_remote_copy(
            src_ref=src, dst_ref=rim_at(0, DIRS.index((-step_r, -step_c))),
            send_sem=send_small.at[0, n], recv_sem=recv_small.at[0, n],
            device_id={"tile": tile + step_r * grid_cols + step_c}, device_id_type=MESH)

    def way(n):
        return 0 if DIRS[n][1] == 0 else 1

    def rim_pass(phase, n):
        return pltpu.make_async_remote_copy(
            src_ref=rim_at(0 if phase == 1 else 3, n), dst_ref=rim_at(phase, n),
            send_sem=send_small.at[phase, n], recv_sem=recv_small.at[phase, n],
            device_id={"group": partners[way(n) if phase == 1 else 1 - way(n)]}, device_id_type=MESH)

    def block_pass(phase, f, k, h):
        cols = pl.ds(pieces[k][0], pieces[k][1] - pieces[k][0])
        rows = pl.ds(h * half, half)
        return pltpu.make_async_remote_copy(
            src_ref=(x_hbm if phase == 1 else relay).at[f, rows, cols],
            dst_ref=(first_in if phase == 1 else second_in).at[f, rows, cols],
            send_sem=send_big.at[phase - 1, f, k, h], recv_sem=recv_big.at[phase - 1, f, k, h],
            device_id={"group": partners[h if phase == 1 else 1 - h]}, device_id_type=MESH)

    def for_dirs(act_on, side=None):
        for n, (step_r, step_c) in enumerate(DIRS):
            if side is None or (step_r == 0) == side:
                pl.when(present(step_r, step_c))(functools.partial(act_on, n))

    def opposite(n):
        return DIRS.index((-DIRS[n][0], -DIRS[n][1]))

    pl.semaphore_wait(barrier, greeted)
    for_dirs(lambda n: rim_copy(n).start(), False)
    for f, k in ((1, 0), (1, 1), (1, 2), (0, 0)):
        for h in (0, 1):
            block_pass(1, f, k, h).start()

    zero_rim = jnp.zeros((pitch, 128), jnp.float32)
    for slot in range(2):
        for c in range(lanes):
            act[slot, c, pl.ds(0, pitch)] = zero_rim
            act[slot, c, pl.ds((core_h + 1) * pitch, pitch)] = zero_rim
            act[slot, c, pl.ds(pitch + 7, core_h, stride=pitch)] = zero_rim[:core_h]
            act[slot, c, pl.ds(pitch + 8 + core_w, core_h, stride=pitch)] = zero_rim[:core_h]

    x_copy.wait()
    for f in range(frames):
        side = x_ref[f].astype(jnp.float32)
        cols_out[0, f] = side[:, 0, :].astype(jnp.bfloat16)
        cols_out[1, f] = side[:, core_w - 1, :].astype(jnp.bfloat16)
    for_dirs(lambda n: rim_copy(n).start(), True)

    for copy in small:
        copy.wait()
    gain = gain_ref[...].reshape(1, channels)
    left, right, up, down = [margin_ref[0, k] for k in range(4)]
    place = slot_ref[group]
    places = [slot_ref[p] for p in partners]
    mine = [jnp.full((1, channels), places[h] == place - 1) for h in (0, 1)]
    theirs = [jnp.full((1, channels), places[h] == places[1 - h] - 1) for h in (0, 1)]

    def choose(hit, a, b):
        return jnp.where(hit, a.astype(jnp.float32), b.astype(jnp.float32))

    not_first = jnp.where(jnp.full((core_h, channels), place > 0), 1.0, 0.0)

    def kept(m):
        m_f = jnp.full((core_h, channels), m, jnp.int32).astype(jnp.float32)
        return (m_f + 1.0) / (m_f + 2.0)

    row_at = lax.broadcasted_iota(jnp.int32, (core_h, channels), 0)
    alpha = [jnp.where(row_at == core_h - down, kept(down), 1.0), None,
             jnp.where(row_at == up - 1, kept(up), 1.0)]
    beta_left = kept(left)
    beta_right = kept(right)

    def put_act(slot, at, v):
        for c in range(lanes):
            act[slot, c, at] = v[:, c * 128:(c + 1) * 128]

    def interior(kind, f, slot, first, last):
        many = half // 2 if last - first > 8 else half

        def some_rows(i, carry):
            for h in (0, 1):
                for k in range(many):
                    row = h * half + many * i + k
                    if kind:
                        v = choose(mine[h], first_in[f, row, first:last], second_in[f, row, first:last])
                    else:
                        v = x_ref[f, row, first:last]
                    at = pl.multiple_of((row + 1) * pitch + 8 + first, 8)
                    put_act(slot, pl.ds(at, last - first), activate(v, gain))
            return carry
        lax.fori_loop(0, half // many, some_rows, 0)

    def forward(f, k):
        first, last = pieces[k]
        for h in (0, 1):
            block_pass(1, f, k, h).wait_recv()

        def some_rows(i, carry):
            for h in (0, 1):
                row = h * half + i
                relay[f, row, first:last] = choose(theirs[h], first_in[f, row, first:last],
                                                   x_ref[f, row, first:last]).astype(jnp.bfloat16)
            return carry
        lax.fori_loop(0, half, some_rows, 0, unroll=2)
        for h in (0, 1):
            block_pass(2, f, k, h).start()

    def forward_rim(n):
        rim_pass(1, n).wait_recv()
        hit = theirs[way(n)]
        for f in range(frames):
            rim_at(3, n)[f] = choose(hit, rim_at(1, n)[f], rim_at(0, n)[f]).astype(jnp.bfloat16)
        rim_pass(2, n).start()

    def rims(kind):
        def one(n):
            step_r, step_c = DIRS[n]
            vertical = (core_h + 1) * pitch if step_r > 0 else 0
            for f in range(frames):
                if kind:
                    v = choose(mine[way(n)], rim_at(1, n)[f], rim_at(2, n)[f])
                else:
                    v = rim_at(0, n)[f]
                v = activate(v, gain)
                if step_c == 0:
                    put_act(f, pl.ds(vertical + 8, core_w), v)
                elif step_r == 0:
                    put_act(f, pl.ds(pitch + (8 + core_w if step_c > 0 else 7), core_h, stride=pitch), v)
                else:
                    put_act(f, pl.ds(vertical + (8 + core_w if step_c > 0 else 7), 1), v[0:1] if step_c > 0 else v[7:8])
        for_dirs(one)

    def column(kind, slot, b, p):
        at = pl.ds(b * pitch + 7 + p, core_h, stride=pitch)
        v = jnp.concatenate([act[slot, c, at] for c in range(lanes)], axis=-1)
        if alpha[b] is not None:
            v = v * alpha[b]
        return v * not_first if kind else v

    def spread(kind, slot, first, last):
        def one_col(p, carry):
            for b in range(3):
                z[slot, b, pl.ds(pl.multiple_of(p * core_h, core_h), core_h)] = column(kind, slot, b, p).astype(jnp.bfloat16)
            return carry
        lax.fori_loop(first, last, one_col, 0, unroll=3)

    def spread_left(kind, slot):
        for j in range(M):
            for b in range(3):
                v = column(kind, slot, b, j + 2)
                edge[slot, b, 1, j * core_h:(j + 1) * core_h] = jnp.where(j == left - 1, v * beta_left, v).astype(jnp.bfloat16)

    def spread_right(kind, slot):
        for j in range(M):
            for b in range(3):
                v = column(kind, slot, b, core_w - M + j)
                edge[slot, b, 0, j * core_h:(j + 1) * core_h] = jnp.where(M - j == right, v * beta_right, v).astype(jnp.bfloat16)

    def spread_all(kind, slot):
        spread(kind, slot, 0, core_w + 2)
        spread_left(kind, slot)
        spread_right(kind, slot)

    def windows(slot, j0, j1):
        def rows(ref, first, last):
            return ref[first * core_h:last * core_h]
        out = []
        for b in range(3):
            plain = z.at[slot, b]
            inner = min(j1, core_w - M)
            near = [rows(plain, j0, inner)]
            if j1 > inner:
                near.append(rows(edge.at[slot, b, 0], 0, j1 - inner))
            outer = max(j0, M)
            far = [rows(edge.at[slot, b, 1], j0, M)] if j0 < M else []
            far.append(rows(plain, outer + 2, j1 + 2))
            out += [jnp.concatenate(near, axis=0), rows(plain, j0 + 1, j1 + 1), jnp.concatenate(far, axis=0)]
        return jnp.concatenate(out, axis=-1)

    def product(slot, first, target, at, j0, j1, whole):
        r = jnp.dot(windows(slot, j0, j1), w[:, pl.ds(pl.multiple_of(first * 128, 128), 256)],
                    preferred_element_type=jnp.float32)

        def left_part():
            acc[target, at] += r[:, :128]
        if whole is None:
            left_part()
        else:
            pl.when(whole)(left_part)
        acc[target + 1, at] += r[:, 128:]

    everything = slice(0, core_h * core_w)

    def at_step(n, turn, act_on):
        pl.when(n == turn)(act_on)

    def forward_next():
        for k in range(3):
            forward(1, k)

    def send_last():
        for_dirs(forward_rim)
        for k in (1, 2):
            for h in (0, 1):
                block_pass(1, 0, k, h).start()
        forward(0, 0)

    def forward_last():
        for k in (1, 2):
            forward(0, k)

    def own_both(n, carry):
        product(0, 2 * n, 2 * n, everything, 0, core_w, None)
        at_step(n, 0, send_last)
        return carry

    def own_single(n, carry):
        product(1, n, lanes + n, everything, 0, core_w, n == 0)
        return carry

    def both_steps(n, carry):
        product(1, lanes + 2 * n, 2 * n, everything, 0, core_w, None)
        at_step(n, 0, functools.partial(forward, 0, 2))
        return carry

    def static_product(slot, first, target, many, j0, j1):
        r = jnp.dot(windows(slot, j0, j1), w[:, first * 128:(first + many) * 128],
                    preferred_element_type=jnp.float32)
        for c in range(many):
            acc[target + c, j0 * core_h:j1 * core_h] += r[:, c * 128:(c + 1) * 128]

    bias = bias_ref[...].reshape(1, channels)

    def give(s, first, last):
        def put(i, carry):
            v = jnp.concatenate([acc[s * lanes + c, pl.ds(i + first * core_h, last - first, stride=core_h)]
                                 for c in range(lanes)], axis=-1)
            out_ref[s, i, first:last] = (v + bias).astype(out_ref.dtype)
            return carry
        lax.fori_loop(0, core_h, put, 0, unroll=8)

    def clear(i, carry):
        acc[i] = jnp.zeros(acc.shape[1:], jnp.float32)
        return carry
    lax.fori_loop(0, 2 * lanes, clear, 0)

    interior(0, 0, 0, 0, core_w)
    interior(0, 1, 1, 0, core_w)
    for_dirs(lambda n: rim_copy(opposite(n)).wait_recv())
    for_dirs(lambda n: rim_pass(1, n).start())
    rims(0)
    for f in (0, 1):
        spread_all(0, f)
        forward(1, f)
    forward(1, 2)
    w_copy(2).wait()
    w_copy(1).wait()
    lax.fori_loop(0, lanes, own_both, 0)
    lax.fori_loop(0, lanes - 1, own_single, 0)

    for k, (first, last) in enumerate(pieces):
        for h in (0, 1):
            block_pass(2, 1, k, h).wait_recv()
        interior(1, 1, 1, first, last)
    for_dirs(lambda n: rim_pass(2, n).wait_recv())
    rims(1)
    spread_all(1, 1)
    w_copy(0).wait()
    forward(0, 1)
    lax.fori_loop(0, lanes, both_steps, 0)
    give(1, 0, core_w)

    def sent(n):
        rim_copy(n).wait_send()
        for phase in (1, 2):
            rim_pass(phase, n).wait_send()
    for_dirs(sent)
    for phase, f in ((1, 1), (2, 1), (1, 0)):
        for k in range(3):
            for h in (0, 1):
                block_pass(phase, f, k, h).wait_send()

    for k in (0, 1):
        for h in (0, 1):
            block_pass(2, 0, k, h).wait_recv()
        interior(1, 0, 0, *pieces[k])
    spread(1, 0, 0, cut + 1)
    spread_left(1, 0)
    for h in (0, 1):
        block_pass(2, 0, 2, h).wait_recv()
    interior(1, 0, 0, cut, core_w)
    spread(1, 0, cut + 1, core_w + 2)
    spread_right(1, 0)
    static_product(0, 2 * lanes, 0, lanes, 0, core_w)
    give(0, 0, core_w)
    for k in range(3):
        for h in (0, 1):
            block_pass(2, 0, k, h).wait_send()


def local(n_group, n_tile, features, group_slot, margins, norm_gain, kernel, conv_bias):
    x = features[0]
    frames, core_h, core_w, channels = x.shape
    weights = kernel.reshape(3, 9 * channels, channels)
    pitch = core_w + 16
    block = pltpu.VMEM((frames, core_h, core_w, channels), jnp.bfloat16)
    vmem = pl.BlockSpec(memory_space=pltpu.VMEM)
    anywhere = pl.BlockSpec(memory_space=pl.ANY)
    out = pl.pallas_call(
        functools.partial(body, n_group, n_tile),
        out_shape=pltpu.VMEM(x.shape, jnp.bfloat16),
        in_specs=[anywhere] * 6,
        out_specs=vmem,
        scratch_shapes=[
            block, block, block, block,
            pltpu.VMEM((4, 2, frames, core_w, channels), jnp.bfloat16),
            pltpu.VMEM((4, 2, frames, core_h, channels), jnp.bfloat16),
            pltpu.VMEM((4, 2, 2, frames, 8, channels), jnp.bfloat16),
            pltpu.VMEM((2, frames, core_h, channels), jnp.bfloat16),
            pltpu.VMEM((9 * channels, 3 * channels), jnp.bfloat16),
            pltpu.VMEM((2, channels // 128, (core_h + 2) * pitch, 128), jnp.float32),
            pltpu.VMEM((2, 3, (core_w + 2) * core_h, channels), jnp.bfloat16),
            pltpu.VMEM((2, 3, 2, M * core_h, channels), jnp.bfloat16),
            pltpu.VMEM((2 * channels // 128, core_h * core_w, 128), jnp.float32),
            pltpu.SemaphoreType.DMA((3, 8)),
            pltpu.SemaphoreType.DMA((3, 8)),
            pltpu.SemaphoreType.DMA((2, 2, 3, 2)),
            pltpu.SemaphoreType.DMA((2, 2, 3, 2)),
            pltpu.SemaphoreType.DMA((3,)),
            pltpu.SemaphoreType.DMA,
            pltpu.SMEM(group_slot.shape, jnp.int32),
            pltpu.SMEM(margins.shape, jnp.int32),
            pltpu.VMEM(norm_gain.shape, jnp.float32),
            pltpu.VMEM(conv_bias.shape, jnp.float32),
            pltpu.SemaphoreType.DMA((4,)),
        ],
        compiler_params=pltpu.CompilerParams(collective_id=0, has_side_effects=True, vmem_limit_bytes=60 << 20),
        name="conv",
    )(group_slot, margins, x, norm_gain, conv_bias, weights)
    return out[None]


def solution(mesh):
    n_group = mesh.shape["group"]
    n_tile = mesh.shape["tile"]
    if n_group != 4:
        raise ValueError("group size")
    return jax.shard_map(
        functools.partial(local, n_group, n_tile),
        mesh=mesh,
        in_specs=(
            P(("video", "tile"), "group", None, None, None),
            P(),
            P("tile", None),
            P(),
            P(),
            P(),
        ),
        out_specs=P(("video", "tile"), "group", None, None, None),
        check_vma=False,
    )
```
